32 devices in a mesh: fsdp: 4 (over z), sp: 8 (over y, x, core).
Axes of the slice: x: 2, y: 2, z: 4, core: 2. Of those that a mesh axis runs over, the one named last changes fastest.
Arguments:
- tokens: bfloat16 [4096, 2048], P(('fsdp', 'sp')), may hold values from -6 to 6
- segments: int32 [4, 1024], P('fsdp'), may hold values from 0 to 7, never falling along the last dimension, each value on 1 to 512 neighbouring positions
- prenorm: bfloat16 [2048], P('fsdp'), may hold values from 0.099609375 to 1.8984375
- query_proj: bfloat16 [2048, 2048], P('fsdp'), may hold values from -0.125 to 0.125
- key_projection: bfloat16 [2048, 1024], P('fsdp'), may hold values from -0.125 to 0.125
- value_projection: bfloat16 [2048, 1024], P('fsdp'), may hold values from -0.125 to 0.125
- query_norm: bfloat16 [128], replicated, may hold values from 0.099609375 to 1.8984375
- key_norm_gain: bfloat16 [128], replicated, may hold values from 0.099609375 to 1.8984375
- output_proj: bfloat16 [2048, 2048], P('fsdp'), may hold values from -1 to 1
- postnorm: bfloat16 [2048], P('fsdp'), may hold values from 0.099609375 to 1.8984375
- gate_proj: bfloat16 [2048, 6144], P('fsdp'), may hold values from -0.125 to 0.125
- up_proj: bfloat16 [2048, 6144], P('fsdp'), may hold values from -0.125 to 0.125
- down_proj: bfloat16 [2048, 6144], P('fsdp'), may hold values from -0.078125 to 0.078125
- out_grad: bfloat16 [4096, 2048], P(('fsdp', 'sp')), may hold values from -6 to 6
Outputs:
- block_out: bfloat16 [4096, 2048], P(('fsdp', 'sp'))
- input_grad: bfloat16 [4096, 2048], P(('fsdp', 'sp'))
- grad_prenorm: float32 [2048], P('fsdp')
- grad_query: float32 [2048, 2048], P('fsdp')
- grad_key: float32 [2048, 1024], P('fsdp')
- grad_value: float32 [2048, 1024], P('fsdp')
- grad_querynorm: float32 [128], replicated
- grad_keynorm: float32 [128], replicated
- grad_output: float32 [2048, 2048], P('fsdp')
- grad_postnorm: float32 [2048], P('fsdp')
- grad_gate: float32 [2048, 6144], P('fsdp')
- grad_up: float32 [2048, 6144], P('fsdp')
- grad_down: float32 [2048, 6144], P('fsdp')
The draws below stay inside these ranges and needn't reach their ends.
Inputs may be any that keep to these rules, and one draw needn't show every extreme that they name: `segments`: document numbers of a sequence's tokens never fall; each of the 8 documents holds 1 to 512 tokens.
All inputs are finite; a program needn't handle non-finite values.
Results may differ from the reference program's by a relative error of at most 0.018.
Values may be sent and summed in bfloat16 or wider, within the bound.
No kernel may reach another device: no remote copies, remote signals or barrier semaphores. Data moves between devices by JAX's collectives and lax.ppermute only.
A program may use at most 384 MiB of HBM per device.

```python
import math
import jax
import jax.numpy as jnp
import numpy as np
from jax import lax

MODEL_DIMENSION = 2048
QUERY_HEADS = 16
KEY_VALUE_HEADS = 8
HEAD_DIMENSION = 128
FF = 6144
DOCS = 8
LEN = 1024
SEQS = 4
TOKENS = 4096


def steps_of(stream_key, extent, cuts, smallest, high):
    def one(axis_at, shards_of):
        steps = jax.random.uniform(jax.random.fold_in(jax.random.fold_in(stream_key, 6), axis_at), (shards_of,), jnp.float32, smallest / len(cuts), high / len(cuts))
        return jnp.repeat(jnp.exp(steps), extent[axis_at] // shards_of).reshape((-1,) + (1,) * (len(extent) - axis_at - 1))

    loudness = one(*cuts[0])
    for cut in cuts[1:]:
        loudness = loudness * one(*cut)
    return loudness


def split_up(count, total, limit, skew):
    portions = [(1 << 20) // math.isqrt(grade ** skew) + 1 for grade in range(2, count + 1)]
    spare, given = total - limit - (count - 1), [1] * (count - 1)
    while spare > 0:
        free = [i for i in range(count - 1) if given[i] < limit]
        mass, left = sum([portions[i] for i in free]), spare
        for i in free:
            extra = min(limit - given[i], max(1, left * portions[i] // mass), spare)
            given[i] = given[i] + extra
            spare = spare - extra
    return np.array([limit] + given)


def ragged_sizes(key, amount, total, most, lean):
    if amount == 2:
        one = jax.random.randint(key, (), max(1, total - most), min(most, total - 1) + 1)
        return jnp.stack([one, total - one])
    lengths = jnp.asarray(split_up(amount, total, most, lean), jnp.int32)
    couples = (amount - 1) // 2
    giver, receiver = lengths[1:1 + 2 * couples:2], lengths[2:2 + 2 * couples:2]
    slack = jnp.minimum(giver - 1, most - receiver)
    moved = jax.random.randint(jax.random.fold_in(key, 1), (couples,), 0, 1 << 20) % (slack + 1)
    lengths = lengths.at[1:1 + 2 * couples:2].set(giver - moved).at[2:2 + 2 * couples:2].set(receiver + moved)
    return lengths[jax.random.permutation(jax.random.fold_in(key, 2), amount)]


def bell_draw(stream_key, dims, deviation, limit, split=(), kind=jnp.bfloat16):
    entries = jax.random.normal(stream_key, dims, jnp.float32) * deviation
    if len(split) > 0:
        entries = steps_of(stream_key, dims, split, -0.22, 0.18) * entries
    return jnp.clip(entries, min=-limit, max=limit).astype(kind)


def setup_inputs(seed: int = 0) -> dict:
    streams_of = jax.random.split(jax.random.key(seed), 15)
    return {
        "tokens": bell_draw(streams_of[0], (TOKENS, MODEL_DIMENSION), 1.0, 6.0, ((0, 32),)),
        "segments": jax.vmap(lambda own: jnp.searchsorted(jnp.cumsum(ragged_sizes(own, DOCS, LEN, LEN // 2, 0)), jnp.arange(LEN), side="right"))(jax.random.split(streams_of[1], SEQS)).reshape((SEQS, LEN)).astype(jnp.int32),
        "prenorm": jnp.clip(1.0 + 0.18 * jax.random.normal(streams_of[2], (MODEL_DIMENSION,), jnp.float32), 0.099609375, 1.8984375).astype(jnp.bfloat16),
        "query_proj": bell_draw(streams_of[3], (MODEL_DIMENSION, QUERY_HEADS * HEAD_DIMENSION), MODEL_DIMENSION ** -0.5, 0.125, ((0, 4),)),
        "key_projection": bell_draw(streams_of[4], (MODEL_DIMENSION, KEY_VALUE_HEADS * HEAD_DIMENSION), MODEL_DIMENSION ** -0.5, 0.125, ((0, 4),)),
        "value_projection": bell_draw(streams_of[5], (MODEL_DIMENSION, KEY_VALUE_HEADS * HEAD_DIMENSION), MODEL_DIMENSION ** -0.5, 0.125, ((0, 4),)),
        "query_norm": jnp.clip(1.0 + 0.18 * jax.random.normal(streams_of[6], (HEAD_DIMENSION,), jnp.float32), 0.099609375, 1.8984375).astype(jnp.bfloat16),
        "key_norm_gain": jnp.clip(1.0 + 0.18 * jax.random.normal(streams_of[7], (HEAD_DIMENSION,), jnp.float32), 0.099609375, 1.8984375).astype(jnp.bfloat16),
        "output_proj": bell_draw(streams_of[8], (QUERY_HEADS * HEAD_DIMENSION, MODEL_DIMENSION), (QUERY_HEADS * HEAD_DIMENSION // 64) ** -0.5, 1.0, ((0, 4),)),
        "postnorm": jnp.clip(1.0 + 0.18 * jax.random.normal(streams_of[9], (MODEL_DIMENSION,), jnp.float32), 0.099609375, 1.8984375).astype(jnp.bfloat16),
        "gate_proj": bell_draw(streams_of[10], (MODEL_DIMENSION, FF), MODEL_DIMENSION ** -0.5, 0.125, ((0, 4),)),
        "up_proj": bell_draw(streams_of[11], (MODEL_DIMENSION, FF), MODEL_DIMENSION ** -0.5, 0.125, ((0, 4),)),
        "down_proj": bell_draw(streams_of[12], (MODEL_DIMENSION, FF), FF ** -0.5, 0.078125, ((0, 4),)),
        "out_grad": bell_draw(streams_of[13], (TOKENS, MODEL_DIMENSION), 1.0, 6.0, ((0, 32),)),
    }


epsilon = 1e-06
rope_base = 1000000.0

def contract_last(left_side, right_side):
    return lax.dot_general(left_side, right_side, (((1,), (1,)), ((), ())), preferred_element_type=jnp.float32)

def contract_first(left_side, right_side):
    return lax.dot_general(left_side, right_side, (((0,), (0,)), ((), ())), preferred_element_type=jnp.float32)

def rope_tables(places):
    half_dim = HEAD_DIMENSION // 2
    frequency = jnp.power(rope_base, -(jnp.arange(half_dim, dtype=jnp.float32) * (2.0 / HEAD_DIMENSION)))
    angles = places[:, None] * frequency[None, :]
    return (jnp.concatenate([jnp.cos(angles), jnp.cos(angles)], axis=1), jnp.concatenate([jnp.sin(angles), jnp.sin(angles)], axis=1))

def rotate(values, cosine, sine_table):
    half_dim = values.shape[-1] // 2
    turned = jnp.concatenate([-values[..., half_dim:], values[..., :half_dim]], axis=-1)
    return values * cosine[:, None, :] + turned * sine_table[:, None, :]

def unrotate(grad_values, cosine, sine_table):
    half_dim = grad_values.shape[-1] // 2
    scaled = grad_values * sine_table[:, None, :]
    turned = jnp.concatenate([scaled[..., half_dim:], -scaled[..., :half_dim]], axis=-1)
    return grad_values * cosine[:, None, :] + turned

def norm_backward(grad_hat, normed, inverse):
    return inverse * (grad_hat - normed * lax.optimization_barrier(jnp.mean(grad_hat * normed, axis=-1, keepdims=True)))

def token_places(seg_row, first_index, tok_count):
    own_segments = lax.dynamic_slice_in_dim(seg_row, first_index, tok_count, 0)
    doc_starts = lax.optimization_barrier(jnp.sum((seg_row[None, :] < own_segments[:, None]).astype(jnp.int32), axis=1))
    positions = first_index + jnp.arange(tok_count, dtype=jnp.int32)
    return (positions - doc_starts).astype(jnp.float32)

def visible(seg_row, first_index, block_len):
    query_place = first_index + jnp.arange(block_len, dtype=jnp.int32)
    key_place = jnp.arange(seg_row.shape[0], dtype=jnp.int32)
    query_seg = lax.dynamic_slice_in_dim(seg_row, first_index, block_len, 0)
    return (key_place[None, :] <= query_place[:, None]) & (seg_row[None, :] == query_seg[:, None])

def attend(query_all, key_all, value_all, seg_row):
    sequence_length = query_all.shape[0]
    block_len = min(512, sequence_length)
    score_scale = HEAD_DIMENSION ** (-0.5)
    key_wide = key_all.astype(jnp.float32)
    value_wide = value_all.astype(jnp.float32)

    def one_block(block_index):
        first_index = block_index * block_len
        query_block = lax.dynamic_slice_in_dim(query_all, first_index, block_len, 0).astype(jnp.float32)
        scores = jnp.einsum('qhd,khd->hqk', query_block, key_wide) * score_scale
        allowed = visible(seg_row, first_index, block_len)
        scores = jnp.where(allowed[None], scores, -1e+30)
        row_top = lax.optimization_barrier(jnp.max(scores, axis=2, keepdims=True))
        log_total = row_top + jnp.log(lax.optimization_barrier(jnp.sum(jnp.exp(scores - row_top), axis=2, keepdims=True)))
        prob_block = jnp.exp(scores - log_total).astype(jnp.bfloat16)
        attended = jnp.einsum('hqk,khd->qhd', prob_block.astype(jnp.float32), value_wide)
        return (attended.astype(jnp.bfloat16), log_total[:, :, 0])
    attended_all, log_totals = lax.map(one_block, jnp.arange(sequence_length // block_len, dtype=jnp.int32))
    return (attended_all.reshape(query_all.shape), log_totals)

def attend_back(query_all, key_all, value_all, attended, out_grads, log_totals, seg_row):
    sequence_length = query_all.shape[0]
    block_len = min(512, sequence_length)
    score_scale = HEAD_DIMENSION ** (-0.5)
    key_wide = key_all.astype(jnp.float32)
    value_wide = value_all.astype(jnp.float32)

    def one_block(state_pair, inputs):
        key_grads, value_grads = state_pair
        block_index, log_total = inputs
        first_index = block_index * block_len
        query_block = lax.dynamic_slice_in_dim(query_all, first_index, block_len, 0).astype(jnp.float32)
        out_block = lax.dynamic_slice_in_dim(attended, first_index, block_len, 0).astype(jnp.float32)
        grad_block = lax.dynamic_slice_in_dim(out_grads, first_index, block_len, 0).astype(jnp.float32)
        scores = jnp.einsum('qhd,khd->hqk', query_block, key_wide) * score_scale
        allowed = visible(seg_row, first_index, block_len)
        prob_block = jnp.where(allowed[None], jnp.exp(scores - log_total[:, :, None]), 0.0)
        rounded = prob_block.astype(jnp.bfloat16).astype(jnp.float32)
        value_grads = value_grads + jnp.einsum('hqk,qhd->khd', rounded, grad_block)
        prob_grads = jnp.einsum('qhd,khd->hqk', grad_block, value_wide)
        row_delta = jnp.transpose(lax.optimization_barrier(jnp.sum(grad_block * out_block, axis=2)))
        score_grads = (prob_block * (prob_grads - row_delta[:, :, None]) * score_scale).astype(jnp.bfloat16).astype(jnp.float32)
        query_grads = jnp.einsum('hqk,khd->qhd', score_grads, key_wide)
        key_grads = key_grads + jnp.einsum('hqk,qhd->khd', score_grads, query_block)
        return ((key_grads, value_grads), query_grads.astype(jnp.bfloat16))
    zero_grads = jnp.zeros(query_all.shape, jnp.float32)
    blocks = jnp.arange(sequence_length // block_len, dtype=jnp.int32)
    (key_grads, value_grads), query_all_grads = lax.scan(one_block, (zero_grads, zero_grads), (blocks, log_totals))
    return (query_all_grads.reshape(query_all.shape), key_grads.astype(jnp.bfloat16), value_grads.astype(jnp.bfloat16))

def one_sequence(tokens, seg_row, out_grad, params):
    prenorm, query_proj, key_projection, value_projection, query_norm, key_norm_gain, output_proj, postnorm, gate_proj, up_proj, down_proj = params
    sequence_length = tokens.shape[0]
    head_repeat_factor = QUERY_HEADS // KEY_VALUE_HEADS
    places = token_places(seg_row, 0, sequence_length)
    cosine, sine_table = rope_tables(places)
    tok_val = tokens.astype(jnp.float32)
    inv_one = lax.rsqrt(lax.optimization_barrier(jnp.mean(tok_val * tok_val, axis=1, keepdims=True)) + epsilon)
    hat_one = tok_val * inv_one
    first_norm = (hat_one * prenorm.astype(jnp.float32)).astype(jnp.bfloat16)
    query_raw = jnp.dot(first_norm, query_proj, preferred_element_type=jnp.float32).reshape(sequence_length, QUERY_HEADS, HEAD_DIMENSION)
    key_unnormalized = jnp.dot(first_norm, key_projection, preferred_element_type=jnp.float32).reshape(sequence_length, KEY_VALUE_HEADS, HEAD_DIMENSION)
    value_unprojected = jnp.dot(first_norm, value_projection, preferred_element_type=jnp.float32).reshape(sequence_length, KEY_VALUE_HEADS, HEAD_DIMENSION)
    query_inv = lax.rsqrt(lax.optimization_barrier(jnp.mean(query_raw * query_raw, axis=2, keepdims=True)) + epsilon)
    query_hat = query_raw * query_inv
    query_rot = rotate(query_hat * query_norm.astype(jnp.float32), cosine, sine_table).astype(jnp.bfloat16)
    key_inverse_norm = lax.rsqrt(lax.optimization_barrier(jnp.mean(key_unnormalized * key_unnormalized, axis=2, keepdims=True)) + epsilon)
    key_normalized = key_unnormalized * key_inverse_norm
    key_rot = rotate(key_normalized * key_norm_gain.astype(jnp.float32), cosine, sine_table).astype(jnp.bfloat16)
    value_head_rows = value_unprojected.astype(jnp.bfloat16)
    key_rep = jnp.repeat(key_rot, head_repeat_factor, axis=1)
    value_rep = jnp.repeat(value_head_rows, head_repeat_factor, axis=1)
    attended, log_totals = attend(query_rot, key_rep, value_rep, seg_row)
    attn_flat = attended.reshape(sequence_length, QUERY_HEADS * HEAD_DIMENSION)
    middle = tok_val + jnp.dot(attn_flat, output_proj, preferred_element_type=jnp.float32)
    inv_two = lax.rsqrt(lax.optimization_barrier(jnp.mean(middle * middle, axis=1, keepdims=True)) + epsilon)
    hat_two = middle * inv_two
    norm_two = (hat_two * postnorm.astype(jnp.float32)).astype(jnp.bfloat16)
    gate_val = jnp.dot(norm_two, gate_proj, preferred_element_type=jnp.float32)
    up_val = jnp.dot(norm_two, up_proj, preferred_element_type=jnp.float32)
    sigmoid_val = jax.nn.sigmoid(gate_val)
    silu_val = gate_val * sigmoid_val
    hidden = (silu_val * up_val).astype(jnp.bfloat16)
    block_out = (middle + contract_last(hidden, down_proj)).astype(jnp.bfloat16)
    grad_down = contract_first(out_grad, hidden)
    hidden_grad = jnp.dot(out_grad, down_proj, preferred_element_type=jnp.float32)
    gate_grad = (hidden_grad * up_val * (sigmoid_val * (1.0 + gate_val * (1.0 - sigmoid_val)))).astype(jnp.bfloat16)
    up_grads = (hidden_grad * silu_val).astype(jnp.bfloat16)
    grad_gate = contract_first(norm_two, gate_grad)
    grad_up = contract_first(norm_two, up_grads)
    norm_two_grad = contract_last(gate_grad, gate_proj) + contract_last(up_grads, up_proj)
    grad_postnorm = lax.optimization_barrier(jnp.sum(norm_two_grad * hat_two, axis=0))
    middle_grad = out_grad.astype(jnp.float32) + norm_backward(norm_two_grad * postnorm.astype(jnp.float32), hat_two, inv_two)
    middle_half = middle_grad.astype(jnp.bfloat16)
    grad_output = contract_first(attn_flat, middle_half)
    attn_grad = contract_last(middle_half, output_proj).astype(jnp.bfloat16).reshape(sequence_length, QUERY_HEADS, HEAD_DIMENSION)
    query_back, key_backward_pass, value_backward_pass = attend_back(query_rot, key_rep, value_rep, attended, attn_grad, log_totals, seg_row)
    key_gradient_sum = lax.optimization_barrier(jnp.sum(key_backward_pass.astype(jnp.float32).reshape(sequence_length, KEY_VALUE_HEADS, head_repeat_factor, HEAD_DIMENSION), axis=2))
    value_gradient_sum = lax.optimization_barrier(jnp.sum(value_backward_pass.astype(jnp.float32).reshape(sequence_length, KEY_VALUE_HEADS, head_repeat_factor, HEAD_DIMENSION), axis=2))
    query_turn = unrotate(query_back.astype(jnp.float32), cosine, sine_table)
    key_rotated = unrotate(key_gradient_sum, cosine, sine_table)
    grad_querynorm = lax.optimization_barrier(jnp.sum(query_turn * query_hat, axis=(0, 1)))
    grad_keynorm = lax.optimization_barrier(jnp.sum(key_rotated * key_normalized, axis=(0, 1)))
    query_lin = norm_backward(query_turn * query_norm.astype(jnp.float32), query_hat, query_inv).reshape(sequence_length, QUERY_HEADS * HEAD_DIMENSION).astype(jnp.bfloat16)
    key_linear = norm_backward(key_rotated * key_norm_gain.astype(jnp.float32), key_normalized, key_inverse_norm).reshape(sequence_length, KEY_VALUE_HEADS * HEAD_DIMENSION).astype(jnp.bfloat16)
    value_linear = value_gradient_sum.reshape(sequence_length, KEY_VALUE_HEADS * HEAD_DIMENSION).astype(jnp.bfloat16)
    grad_query = contract_first(first_norm, query_lin)
    grad_key = contract_first(first_norm, key_linear)
    grad_value = contract_first(first_norm, value_linear)
    norm_one_grad = contract_last(query_lin, query_proj) + contract_last(key_linear, key_projection) + contract_last(value_linear, value_projection)
    grad_prenorm = lax.optimization_barrier(jnp.sum(norm_one_grad * hat_one, axis=0))
    input_grad = (middle_grad + norm_backward(norm_one_grad * prenorm.astype(jnp.float32), hat_one, inv_one)).astype(jnp.bfloat16)
    gradients = (grad_prenorm, grad_query, grad_key, grad_value, grad_querynorm, grad_keynorm, grad_output, grad_postnorm, grad_gate, grad_up, grad_down)
    return (block_out, input_grad, gradients)

def reference(tokens, segments, prenorm, query_proj, key_projection, value_projection, query_norm, key_norm_gain, output_proj, postnorm, gate_proj, up_proj, down_proj, out_grad):
    params = (prenorm, query_proj, key_projection, value_projection, query_norm, key_norm_gain, output_proj, postnorm, gate_proj, up_proj, down_proj)
    seq_tokens = tokens.reshape(SEQS, LEN, MODEL_DIMENSION)
    seq_grads = out_grad.reshape(SEQS, LEN, MODEL_DIMENSION)

    def step(totals, item):
        tok_seq, seg_seq, grad_seq = item
        block_out, input_grad, gradients = one_sequence(tok_seq, seg_seq, grad_seq, params)
        return (tuple((total + part for total, part in zip(totals, gradients))), (block_out, input_grad))
    start_totals = tuple((jnp.zeros(weight.shape, jnp.float32) for weight in params))
    totals, (outputs, input_grads) = lax.scan(step, start_totals, (seq_tokens, segments, seq_grads))
    return (outputs.reshape(TOKENS, MODEL_DIMENSION), input_grads.reshape(TOKENS, MODEL_DIMENSION), totals[0], totals[1], totals[2], totals[3], totals[4], totals[5], totals[6], totals[7], totals[8], totals[9], totals[10])
```

```python
import jax
import jax.numpy as jnp
from jax import lax
from jax.sharding import PartitionSpec as P

QUERY_HEADS = 16
KEY_VALUE_HEADS = 8
HEAD_DIMENSION = 128


epsilon = 1e-06
rope_base = 1000000.0
single_precision = jnp.float32
reduced_precision = jnp.bfloat16


def contract_last(left_side, right_side):
    return lax.dot_general(
        left_side, right_side, (((1,), (1,)), ((), ())), preferred_element_type=single_precision
    )


def contract_first(left_side, right_side):
    return lax.dot_general(
        left_side, right_side, (((0,), (0,)), ((), ())), preferred_element_type=single_precision
    )


def rope_tables(places):
    half_dim = HEAD_DIMENSION // 2
    frequency = jnp.power(
        rope_base, -(jnp.arange(half_dim, dtype=single_precision) * (2.0 / HEAD_DIMENSION))
    )
    angles = places[:, None] * frequency[None, :]
    return (
        jnp.concatenate([jnp.cos(angles), jnp.cos(angles)], axis=1),
        jnp.concatenate([jnp.sin(angles), jnp.sin(angles)], axis=1),
    )


def rotate(values, cosine, sine_table):
    half_dim = values.shape[-1] // 2
    turned = jnp.concatenate([-values[..., half_dim:], values[..., :half_dim]], axis=-1)
    return values * cosine[:, None, :] + turned * sine_table[:, None, :]


def unrotate(grad_values, cosine, sine_table):
    half_dim = grad_values.shape[-1] // 2
    scaled = grad_values * sine_table[:, None, :]
    turned = jnp.concatenate([scaled[..., half_dim:], -scaled[..., :half_dim]], axis=-1)
    return grad_values * cosine[:, None, :] + turned


def norm_backward(grad_hat, normed, inverse):
    return inverse * (grad_hat - normed * jnp.mean(grad_hat * normed, axis=-1, keepdims=True))


def token_places(seg_row, first_index, tok_count):
    own_segments = lax.dynamic_slice_in_dim(seg_row, first_index, tok_count, 0)
    doc_starts = jnp.sum((seg_row[None, :] < own_segments[:, None]).astype(jnp.int32), axis=1)
    positions = first_index + jnp.arange(tok_count, dtype=jnp.int32)
    return (positions - doc_starts).astype(single_precision)


def visible(seg_row, first_index, block_len):
    query_place = first_index + jnp.arange(block_len, dtype=jnp.int32)
    key_place = jnp.arange(seg_row.shape[0], dtype=jnp.int32)
    query_seg = lax.dynamic_slice_in_dim(seg_row, first_index, block_len, 0)
    return (key_place[None, :] <= query_place[:, None]) & (seg_row[None, :] == query_seg[:, None])


def attend(query_heads, key_heads, value_head_rows, seg_row, block_len):
    sequence_length = query_heads.shape[0]
    score_scale = HEAD_DIMENSION ** (-0.5)

    def one_block(block_index):
        first_index = block_index * block_len
        query_block = lax.dynamic_slice_in_dim(query_heads, first_index, block_len, 0)
        scores = (
            jnp.einsum(
                "qhd,khd->hqk", query_block, key_heads, preferred_element_type=single_precision
            )
            * score_scale
        )
        allowed = visible(seg_row, first_index, block_len)
        scores = jnp.where(allowed[None], scores, -1e30)
        row_top = jnp.max(scores, axis=2, keepdims=True)
        log_total = row_top + jnp.log(jnp.sum(jnp.exp(scores - row_top), axis=2, keepdims=True))
        prob_block = jnp.exp(scores - log_total).astype(reduced_precision)
        attended = jnp.einsum(
            "hqk,khd->qhd", prob_block, value_head_rows, preferred_element_type=single_precision
        )
        return (attended.astype(reduced_precision), log_total[:, :, 0])

    attended_all, log_totals = lax.map(
        one_block, jnp.arange(sequence_length // block_len, dtype=jnp.int32)
    )
    return (attended_all.reshape(query_heads.shape), log_totals)


def attend_back(
    query_heads, key_heads, value_head_rows, attended, out_grads, log_totals, seg_row, block_len
):
    sequence_length = query_heads.shape[0]
    score_scale = HEAD_DIMENSION ** (-0.5)

    def one_block(state_pair, inputs):
        key_grads, value_grads = state_pair
        block_index, log_total = inputs
        first_index = block_index * block_len
        query_block = lax.dynamic_slice_in_dim(query_heads, first_index, block_len, 0)
        out_block = lax.dynamic_slice_in_dim(attended, first_index, block_len, 0)
        grad_block = lax.dynamic_slice_in_dim(out_grads, first_index, block_len, 0)
        scores = (
            jnp.einsum(
                "qhd,khd->hqk", query_block, key_heads, preferred_element_type=single_precision
            )
            * score_scale
        )
        allowed = visible(seg_row, first_index, block_len)
        prob_block = jnp.where(allowed[None], jnp.exp(scores - log_total[:, :, None]), 0.0)
        rounded = prob_block.astype(reduced_precision)
        value_grads = value_grads + jnp.einsum(
            "hqk,qhd->khd", rounded, grad_block, preferred_element_type=single_precision
        )
        prob_grads = jnp.einsum(
            "qhd,khd->hqk", grad_block, value_head_rows, preferred_element_type=single_precision
        )
        row_delta = jnp.transpose(
            jnp.sum(
                grad_block.astype(single_precision) * out_block.astype(single_precision), axis=2
            )
        )
        score_grads = (prob_block * (prob_grads - row_delta[:, :, None]) * score_scale).astype(
            reduced_precision
        )
        query_grads = jnp.einsum(
            "hqk,khd->qhd", score_grads, key_heads, preferred_element_type=single_precision
        )
        key_grads = key_grads + jnp.einsum(
            "hqk,qhd->khd", score_grads, query_block, preferred_element_type=single_precision
        )
        return ((key_grads, value_grads), query_grads.astype(reduced_precision))

    zero_grads = jnp.zeros(query_heads.shape, single_precision)
    blocks = jnp.arange(sequence_length // block_len, dtype=jnp.int32)
    (key_grads, value_grads), query_all = lax.scan(
        one_block, (zero_grads, zero_grads), (blocks, log_totals)
    )
    return (
        query_all.reshape(query_heads.shape),
        key_grads.astype(reduced_precision),
        value_grads.astype(reduced_precision),
    )


def plane_permute(piece, flip):
    size = lax.axis_size("sp")
    return lax.ppermute(piece, "sp", [(i, i ^ flip) for i in range(size)])


def plane_gather(piece):
    size = lax.axis_size("sp")
    if size != 8:
        return lax.all_gather(piece, "sp", axis=0)
    index = lax.axis_index("sp")
    chip, core = index // 2, index % 2
    found = [piece] + [plane_permute(piece, 2 * turn) for turn in (1, 2, 3)]
    mine = jnp.zeros((4,) + piece.shape, piece.dtype)
    for turn, part in enumerate(found):
        mine = lax.dynamic_update_index_in_dim(mine, part, chip ^ turn, 0)
    other = plane_permute(mine, 1)
    even = jnp.where(core == 0, mine, other)
    odd = jnp.where(core == 0, other, mine)
    return jnp.stack([even, odd], axis=1).reshape((8,) + piece.shape)


def plane_reduce(parts):
    size = lax.axis_size("sp")
    if size != 8:
        return lax.psum_scatter(parts, "sp", scatter_dimension=0, tiled=False).astype(
            single_precision
        )
    index = lax.axis_index("sp")
    chip, core = index // 2, index % 2
    split = parts.reshape((4, 2) + parts.shape[1:])
    given = lax.dynamic_index_in_dim(split, 1 - core, 1, keepdims=False)
    kept = lax.dynamic_index_in_dim(split, core, 1, keepdims=False)
    joined = (
        kept.astype(single_precision) + plane_permute(given, 1).astype(single_precision)
    ).astype(reduced_precision)
    total = lax.dynamic_index_in_dim(joined, chip, 0, keepdims=False).astype(single_precision)
    for turn in (1, 2, 3):
        sent = lax.dynamic_index_in_dim(joined, chip ^ turn, 0, keepdims=False)
        total = total + plane_permute(sent, 2 * turn).astype(single_precision)
    return total


def line_reduce(parts):
    size = lax.axis_size("fsdp")
    if size < 3:
        return lax.psum_scatter(parts, "fsdp", scatter_dimension=0, tiled=False)
    index = lax.axis_index("fsdp")

    def own(at):
        return lax.dynamic_index_in_dim(parts, at % size, 0, keepdims=False)

    def plus(left, right):
        return (left.astype(single_precision) + right.astype(single_precision)).astype(
            parts.dtype
        )

    first = own(jnp.where(index == 0, size - 1, 0))
    up = lax.ppermute(first, "fsdp", [(0, 1), (size - 1, size - 2)])
    down = up
    for step in range(2, size):
        up = lax.ppermute(
            plus(own(index + size - step), up), "fsdp", [(i, i + 1) for i in range(step)]
        )
        down = lax.ppermute(
            plus(own(index + step), down),
            "fsdp",
            [(i, i - 1) for i in range(size - step, size)],
        )
    return (
        own(index).astype(single_precision)
        + up.astype(single_precision)
        + down.astype(single_precision)
    ).astype(parts.dtype)


def columns_of(weight, first, width):
    return lax.dynamic_slice_in_dim(weight, first, width, 1)


def spread(reduced, widths):
    size = lax.axis_size("sp")
    everything = lax.all_gather(reduced, "sp", axis=0)
    rows = reduced.shape[0]
    results = []
    offset = 0
    for width in widths:
        piece = everything[:, :, offset : offset + width].astype(single_precision)
        results.append(jnp.transpose(piece, (1, 0, 2)).reshape(rows, size * width))
        offset = offset + width
    return results


def on_device(
    tokens,
    segments,
    prenorm,
    query_proj,
    key_projection,
    value_projection,
    query_norm,
    key_norm_gain,
    output_proj,
    postnorm,
    gate_proj,
    up_proj,
    down_proj,
    out_grad,
):
    token_rows, model_width = tokens.shape
    plane = lax.axis_size("sp")
    lines = lax.axis_size("fsdp")
    spot = lax.axis_index("sp")
    seg_row = segments[0]
    length = seg_row.shape[0]
    block_len = min(512, length)
    local_heads = QUERY_HEADS // plane
    query_width = local_heads * HEAD_DIMENSION
    share = max(1, plane // KEY_VALUE_HEADS)
    owned = HEAD_DIMENSION // share
    model_cols = model_width // plane
    ff_cols = gate_proj.shape[1] // plane
    row_block = model_width // lines

    everyone = plane_gather(tokens).reshape(length, model_width)
    gains = lax.all_gather(jnp.stack([prenorm, postnorm]), "fsdp", axis=1, tiled=True)
    prenorm_full = gains[0].astype(single_precision)
    postnorm_full = gains[1].astype(single_precision)
    kv_first = (spot // share) * HEAD_DIMENSION
    qkv_slice = jnp.concatenate(
        [
            columns_of(query_proj, spot * query_width, query_width),
            columns_of(key_projection, kv_first, HEAD_DIMENSION),
            columns_of(value_projection, kv_first, HEAD_DIMENSION),
        ],
        axis=1,
    )
    qkv = lax.all_gather(qkv_slice, "fsdp", axis=0, tiled=True)
    out_cols = lax.all_gather(
        columns_of(output_proj, spot * model_cols, model_cols), "fsdp", axis=0, tiled=True
    )
    gate_up = lax.all_gather(
        jnp.concatenate(
            [
                columns_of(gate_proj, spot * ff_cols, ff_cols),
                columns_of(up_proj, spot * ff_cols, ff_cols),
            ],
            axis=1,
        ),
        "fsdp",
        axis=0,
        tiled=True,
    )
    down_cols = lax.all_gather(
        columns_of(down_proj, spot * ff_cols, ff_cols), "fsdp", axis=0, tiled=True
    )

    places = token_places(seg_row, 0, length)
    cosine, sine_table = rope_tables(places)
    tok_val = everyone.astype(single_precision)
    inv_one = lax.rsqrt(jnp.mean(tok_val * tok_val, axis=1, keepdims=True) + epsilon)
    first_norm = (tok_val * inv_one * prenorm_full[None, :]).astype(reduced_precision)
    raw = jnp.dot(first_norm, qkv, preferred_element_type=single_precision)
    query_raw = raw[:, :query_width].reshape(length, local_heads, HEAD_DIMENSION)
    key_raw = raw[:, query_width : query_width + HEAD_DIMENSION].reshape(length, 1, HEAD_DIMENSION)
    value_one = raw[:, query_width + HEAD_DIMENSION :].astype(reduced_precision)
    query_inv = lax.rsqrt(jnp.mean(query_raw * query_raw, axis=2, keepdims=True) + epsilon)
    query_hat = query_raw * query_inv
    query_rot = rotate(query_hat * query_norm.astype(single_precision), cosine, sine_table).astype(
        reduced_precision
    )
    key_inv = lax.rsqrt(jnp.mean(key_raw * key_raw, axis=2, keepdims=True) + epsilon)
    key_hat = key_raw * key_inv
    key_rot = rotate(key_hat * key_norm_gain.astype(single_precision), cosine, sine_table).astype(
        reduced_precision
    )
    key_heads = jnp.repeat(key_rot, local_heads, axis=1)
    value_heads = jnp.repeat(value_one.reshape(length, 1, HEAD_DIMENSION), local_heads, axis=1)
    attended, log_totals = attend(query_rot, key_heads, value_heads, seg_row, block_len)
    attn_all = plane_gather(attended.reshape(length, query_width))
    attn_all = jnp.transpose(attn_all, (1, 0, 2)).reshape(length, model_width)
    middle_cols = columns_of(everyone, spot * model_cols, model_cols).astype(
        single_precision
    ) + jnp.dot(attn_all, out_cols, preferred_element_type=single_precision)
    middle_all = plane_gather(middle_cols.astype(reduced_precision))
    middle_all = jnp.transpose(middle_all, (1, 0, 2)).reshape(length, model_width)
    middle = middle_all.astype(single_precision)
    inv_two = lax.rsqrt(jnp.mean(middle * middle, axis=1, keepdims=True) + epsilon)
    second_norm = (middle * inv_two * postnorm_full[None, :]).astype(reduced_precision)
    middle_own = lax.dynamic_slice_in_dim(
        middle_all, spot * token_rows, token_rows, 0
    ).astype(single_precision)
    inv_two_own = lax.dynamic_slice_in_dim(inv_two, spot * token_rows, token_rows, 0)
    hat_two_own = middle_own * inv_two_own

    grads_all = plane_gather(out_grad).reshape(length, model_width)
    gate_up_val = jnp.dot(second_norm, gate_up, preferred_element_type=single_precision)
    gate_val = gate_up_val[:, :ff_cols]
    up_val = gate_up_val[:, ff_cols:]
    sigmoid_val = jax.nn.sigmoid(gate_val)
    silu_val = gate_val * sigmoid_val
    hidden = (silu_val * up_val).astype(reduced_precision)
    down_part = contract_first(grads_all, hidden).astype(reduced_precision)
    down_sum = line_reduce(down_part.reshape(lines, row_block, ff_cols))
    hidden_grad = jnp.dot(grads_all, down_cols, preferred_element_type=single_precision)
    gate_grad = (
        hidden_grad * up_val * (sigmoid_val * (1.0 + gate_val * (1.0 - sigmoid_val)))
    ).astype(reduced_precision)
    up_grads = (hidden_grad * silu_val).astype(reduced_precision)
    both_grads = jnp.concatenate([gate_grad, up_grads], axis=1)
    norm_two_part = contract_last(both_grads, gate_up).astype(reduced_precision)
    norm_two_grad = plane_reduce(norm_two_part.reshape(plane, token_rows, model_width))
    gate_up_part = contract_first(second_norm, both_grads).astype(reduced_precision)
    gate_up_sum = line_reduce(gate_up_part.reshape(lines, row_block, 2 * ff_cols))
    block_part = contract_last(hidden, down_cols).astype(reduced_precision)
    block_out = (
        middle_own + plane_reduce(block_part.reshape(plane, token_rows, model_width))
    ).astype(reduced_precision)

    postnorm_part = jnp.sum(norm_two_grad * hat_two_own, axis=0)
    middle_grad = out_grad.astype(single_precision) + norm_backward(
        norm_two_grad * postnorm_full, hat_two_own, inv_two_own
    )
    half_all = plane_gather(middle_grad.astype(reduced_precision)).reshape(length, model_width)
    out_part = contract_first(
        attn_all, columns_of(half_all, spot * model_cols, model_cols)
    ).astype(reduced_precision)
    out_rows = lax.all_to_all(
        out_cols.reshape(plane, query_width, model_cols), "sp", split_axis=0, concat_axis=0, tiled=True
    )
    out_rows = jnp.transpose(
        out_rows.reshape(plane, query_width, model_cols), (1, 0, 2)
    ).reshape(query_width, model_width)
    attn_grad = contract_last(half_all, out_rows).astype(reduced_precision)
    query_back, key_back, value_back = attend_back(
        query_rot,
        key_heads,
        value_heads,
        attended,
        attn_grad.reshape(length, local_heads, HEAD_DIMENSION),
        log_totals,
        seg_row,
        block_len,
    )
    query_turn = unrotate(query_back.astype(single_precision), cosine, sine_table)
    key_sum = jnp.sum(key_back.astype(single_precision), axis=1, keepdims=True)
    value_sum = jnp.sum(value_back.astype(single_precision), axis=1)
    if share > 1:
        groups = [
            [first + offset for offset in range(share)] for first in range(0, plane, share)
        ]
        both = jnp.concatenate([key_sum[:, 0], value_sum], axis=1)
        gathered = [both]
        for turn in range(1, share):
            pairs = [
                (group[i], group[(i + turn) % share]) for group in groups for i in range(share)
            ]
            gathered.append(lax.ppermute(both, "sp", pairs))
        both = sum(gathered[1:], gathered[0])
        key_sum = both[:, None, :HEAD_DIMENSION]
        value_sum = both[:, HEAD_DIMENSION:]
    key_turn = unrotate(key_sum, cosine, sine_table)
    querynorm_part = jnp.sum(query_turn * query_hat, axis=(0, 1))
    keynorm_part = jnp.sum(key_turn * key_hat, axis=(0, 1)) / share
    query_lin = (
        norm_backward(query_turn * query_norm.astype(single_precision), query_hat, query_inv)
        .reshape(length, query_width)
        .astype(reduced_precision)
    )
    key_lin = (
        norm_backward(key_turn * key_norm_gain.astype(single_precision), key_hat, key_inv)
        .reshape(length, HEAD_DIMENSION)
        .astype(reduced_precision)
    )
    value_lin = value_sum.astype(reduced_precision)
    if share > 1:
        own_first = (spot % share) * owned
        key_lin = columns_of(key_lin, own_first, owned)
        value_lin = columns_of(value_lin, own_first, owned)
        qkv = jnp.concatenate(
            [
                qkv[:, :query_width],
                columns_of(qkv, query_width + own_first, owned),
                columns_of(qkv, query_width + HEAD_DIMENSION + own_first, owned),
            ],
            axis=1,
        )
    lin = jnp.concatenate([query_lin, key_lin, value_lin], axis=1)
    norm_one_part = contract_last(lin, qkv).astype(reduced_precision)
    qkv_part = contract_first(first_norm, lin).astype(reduced_precision)
    attn_part = jnp.concatenate([qkv_part, out_part], axis=1)
    attn_sum = line_reduce(attn_part.reshape(lines, row_block, attn_part.shape[1]))
    norm_one_grad = plane_reduce(norm_one_part.reshape(plane, token_rows, model_width))
    own_tok = tokens.astype(single_precision)
    inv_own = lax.rsqrt(jnp.mean(own_tok * own_tok, axis=1, keepdims=True) + epsilon)
    hat_own = own_tok * inv_own
    prenorm_part = jnp.sum(norm_one_grad * hat_own, axis=0)
    input_grad = (
        middle_grad + norm_backward(norm_one_grad * prenorm_full, hat_own, inv_own)
    ).astype(reduced_precision)
    small = lax.psum(
        jnp.concatenate([prenorm_part, postnorm_part, querynorm_part, keynorm_part]),
        ("fsdp", "sp"),
    )
    row_first = lax.axis_index("fsdp") * row_block
    grad_prenorm = lax.dynamic_slice_in_dim(small, row_first, row_block, 0)
    grad_postnorm = lax.dynamic_slice_in_dim(small, model_width + row_first, row_block, 0)
    grad_querynorm = small[2 * model_width : 2 * model_width + HEAD_DIMENSION]
    grad_keynorm = small[2 * model_width + HEAD_DIMENSION :]
    (grad_down,) = spread(down_sum, [ff_cols])
    grad_gate, grad_up = spread(gate_up_sum, [ff_cols, ff_cols])
    grad_query, grad_key, grad_value, grad_output = spread(
        attn_sum, [query_width, owned, owned, model_cols]
    )
    return (
        block_out,
        input_grad,
        grad_prenorm,
        grad_query,
        grad_key,
        grad_value,
        grad_querynorm,
        grad_keynorm,
        grad_output,
        grad_postnorm,
        grad_gate,
        grad_up,
        grad_down,
    )


def solution(mesh):
    placed = (
        P(("fsdp", "sp"), None),
        P("fsdp", None),
        P("fsdp"),
        P("fsdp", None),
        P("fsdp", None),
        P("fsdp", None),
        P(),
        P(),
        P("fsdp", None),
        P("fsdp"),
        P("fsdp", None),
        P("fsdp", None),
        P("fsdp", None),
        P(("fsdp", "sp"), None),
    )
    return jax.shard_map(
        on_device,
        mesh=mesh,
        in_specs=placed,
        out_specs=(
            P(("fsdp", "sp"), None),
            P(("fsdp", "sp"), None),
            P("fsdp"),
            P("fsdp", None),
            P("fsdp", None),
            P("fsdp", None),
            P(),
            P(),
            P("fsdp", None),
            P("fsdp"),
            P("fsdp", None),
            P("fsdp", None),
            P("fsdp", None),
        ),
        check_vma=False,
    )
```

```python
import functools

import jax
import jax.numpy as jnp
from jax import lax
from jax.experimental import pallas as pl
from jax.experimental.layout import Layout, with_layout_constraint
from jax.experimental.pallas import tpu as pltpu
from jax.sharding import PartitionSpec as P


QUERY_HEADS = 16
KEY_VALUE_HEADS = 8
HEAD_DIMENSION = 128
LINE = 4
PLANE = 8
FSDP = "fsdp"
SP = "sp"

epsilon = 1e-06
rope_base = 1000000.0
single_precision = jnp.float32
reduced_precision = jnp.bfloat16


def contract_last(left_side, right_side):
    return lax.dot_general(
        left_side, right_side, (((1,), (1,)), ((), ())), preferred_element_type=single_precision
    )


def contract_first(left_side, right_side):
    return lax.dot_general(
        left_side, right_side, (((0,), (0,)), ((), ())), preferred_element_type=single_precision
    )


def matmul(left_side, right_side):
    return jnp.dot(left_side, right_side, preferred_element_type=single_precision)


def tie(*values):
    return lax.optimization_barrier(values)


def rope_tables(places):
    half_dim = HEAD_DIMENSION // 2
    frequency = jnp.power(
        rope_base, -(jnp.arange(half_dim, dtype=single_precision) * (2.0 / HEAD_DIMENSION))
    )
    angles = places[:, None] * frequency[None, :]
    cosine, sine = jnp.cos(angles), jnp.sin(angles)
    return jnp.concatenate([cosine, cosine], axis=1), jnp.concatenate([-sine, sine], axis=1)


def rotate(values, cosine, signed_sine):
    return values * cosine + pltpu.roll(values, HEAD_DIMENSION // 2, 1) * signed_sine


def unrotate(values, cosine, signed_sine):
    return values * cosine - pltpu.roll(values, HEAD_DIMENSION // 2, 1) * signed_sine


def inverse_norm(values):
    return lax.rsqrt(jnp.mean(values * values, axis=-1, keepdims=True) + epsilon)


def norm_backward(grad_hat, normed, inverse):
    return inverse * (grad_hat - normed * jnp.mean(grad_hat * normed, axis=-1, keepdims=True))


def token_places(seg_row):
    doc_starts = jnp.sum((seg_row[None, :] < seg_row[:, None]).astype(jnp.int32), axis=1)
    positions = jnp.arange(seg_row.shape[0], dtype=jnp.int32)
    return (positions - doc_starts).astype(single_precision)


def flip_permute(piece, axis, flip):
    size = lax.axis_size(axis)
    return lax.ppermute(piece, axis, [(i, i ^ flip) for i in range(size)])


def line_order(blocks):
    if len(blocks) != LINE:
        return blocks
    index = lax.axis_index(FSDP)
    odd, high = index % 2 == 1, index // 2 == 1
    near = [jnp.where(odd, blocks[i ^ 1], blocks[i]) for i in range(LINE)]
    return [jnp.where(high, near[i ^ 2], near[i]) for i in range(LINE)]


def line_columns(values):
    lines = lax.axis_size(FSDP)
    if lines != LINE:
        return values
    return jnp.concatenate(line_order(jnp.split(values, lines, axis=1)), axis=1)


def line_gather(piece):
    if lax.axis_size(FSDP) != LINE:
        return list(lax.all_gather(piece, FSDP, axis=0))
    index = lax.axis_index(FSDP)
    second = flip_permute(piece, FSDP, 2)
    first = flip_permute(piece, FSDP, 1)
    inner = lax.ppermute(piece, FSDP, [(1, 2), (2, 1)])
    outer = lax.ppermute(second, FSDP, [(2, 3), (1, 0)])
    third = jnp.where((index == 1) | (index == 2), inner, outer)
    return [piece, first, second, third]


def line_reduce(parts):
    if lax.axis_size(FSDP) != LINE:
        return lax.psum_scatter(jnp.stack(parts), FSDP, scatter_dimension=0, tiled=False)

    def wide(part):
        return part.astype(single_precision)

    kind = parts[0].dtype
    outer = lax.ppermute(parts[3], FSDP, [(3, 2), (0, 1)])
    inner = lax.ppermute(parts[3], FSDP, [(1, 2), (2, 1)])
    first = flip_permute(parts[1], FSDP, 1)
    second = flip_permute((wide(parts[2]) + wide(outer)).astype(kind), FSDP, 2)
    return (wide(parts[0]) + wide(first) + wide(inner) + wide(second)).astype(kind)


def row_parts(left, right):
    parts = []
    for block in jnp.split(left, lax.axis_size(FSDP), axis=1):
        parts.append(contract_first(block, right).astype(reduced_precision))
    return parts


def unsummed(parts):
    return parts[:2] + parts[3:]


def plane_rows(piece):
    return lax.all_gather(piece, SP, axis=0, tiled=True)


def joining_kernel(count, order, *refs):
    pieces, gain, outs = refs[:count], refs[count], refs[count + 1 :]
    whole = jnp.concatenate([piece[0] for piece in pieces], axis=1)
    outs[0][...] = whole
    if len(outs) > 1:
        wide = whole.astype(single_precision)
        outs[1][...] = (wide * inverse_norm(wide) * gain[...]).astype(reduced_precision)


def plane_columns(piece, gain, normed):
    plane, lines = lax.axis_size(SP), lax.axis_size(FSDP)
    pieces = lax.all_gather(piece, SP, axis=0)
    rows, width = piece.shape
    order = jnp.arange(plane, dtype=jnp.int32)
    if lines == LINE:
        order = order ^ (lax.axis_index(FSDP) * (plane // lines))
    tile = 128

    def from_piece(at):
        return pl.BlockSpec((1, tile, width), lambda row, order: (order[at], row, 0))

    whole = pl.BlockSpec((tile, plane * width), lambda row, order: (row, 0))
    count = 2 if normed else 1
    return pl.pallas_call(
        functools.partial(joining_kernel, plane),
        out_shape=[jax.ShapeDtypeStruct((rows, plane * width), piece.dtype)] * count,
        grid_spec=pltpu.PrefetchScalarGridSpec(
            num_scalar_prefetch=1,
            grid=(rows // tile,),
            in_specs=[from_piece(at) for at in range(plane)]
            + [pl.BlockSpec((1, plane * width), lambda row, order: (0, 0))],
            out_specs=[whole] * count,
        ),
    )(order, *[pieces] * plane, gain)


def plane_reduce(parts):
    if lax.axis_size(SP) != PLANE:
        return lax.psum_scatter(parts, SP, scatter_dimension=0, tiled=False).astype(
            single_precision
        )
    index = lax.axis_index(SP)
    chip, core = index // 2, index % 2
    split = parts.reshape((4, 2) + parts.shape[1:])
    given = lax.dynamic_index_in_dim(split, 1 - core, 1, keepdims=False)
    kept = lax.dynamic_index_in_dim(split, core, 1, keepdims=False)
    other = flip_permute(given, SP, 1)
    joined = (kept.astype(single_precision) + other.astype(single_precision)).astype(
        reduced_precision
    )
    total = lax.dynamic_index_in_dim(joined, chip, 0, keepdims=False).astype(single_precision)
    for turn in (1, 2, 3):
        sent = lax.dynamic_index_in_dim(joined, chip ^ turn, 0, keepdims=False)
        found = flip_permute(sent, SP, 2 * turn)
        total = total + found.astype(single_precision)
    return total


def columns_of(weight, first, width):
    return lax.dynamic_slice_in_dim(weight, first, width, 1)


def widening_kernel(widths, piece, *outs):
    offset = 0
    for width, out in zip(widths, outs):
        out[...] = piece[0, :, offset : offset + width].astype(out.dtype)
        offset = offset + width


def spread(reduced, widths):
    size = lax.axis_size(SP)
    rows, total = reduced.shape
    reduced = with_layout_constraint(reduced, Layout(major_to_minor=(0, 1)))
    everything = lax.all_gather(reduced, SP, axis=0)
    tile = 256
    if all(width % 128 == 0 for width in widths) and rows % tile == 0:
        return pl.pallas_call(
            functools.partial(widening_kernel, widths),
            grid=(rows // tile, size),
            out_shape=[
                jax.ShapeDtypeStruct((rows, size * width), single_precision)
                for width in widths
            ],
            in_specs=[pl.BlockSpec((1, tile, total), lambda row, at: (at, row, 0))],
            out_specs=[pl.BlockSpec((tile, width), lambda row, at: (row, at)) for width in widths],
        )(everything)
    results = []
    offset = 0
    for width in widths:
        piece = everything[:, :, offset : offset + width].astype(single_precision)
        results.append(jnp.transpose(piece, (1, 0, 2)).reshape(rows, size * width))
        offset = offset + width
    return results


def projecting_kernel(heads, count, x, gain, query_gain, key_gain, cosine, sine, *refs):
    blocks, (normed_out, raw_out, turned_out) = refs[:count], refs[count:]
    wide = x[...].astype(single_precision)
    normed = (wide * inverse_norm(wide) * gain[...]).astype(reduced_precision)
    normed_out[...] = normed
    depth = blocks[0].shape[0]
    total = matmul(normed[:, :depth], blocks[0][...])
    for at in range(1, count):
        total = total + matmul(normed[:, at * depth : (at + 1) * depth], blocks[at][...])
    raw_out[...] = total[:, : (heads + 1) * HEAD_DIMENSION]
    for head in range(heads + 2):
        window = slice(head * HEAD_DIMENSION, (head + 1) * HEAD_DIMENSION)
        values = total[:, window]
        if head <= heads:
            head_gain = query_gain if head < heads else key_gain
            values = rotate(
                values * inverse_norm(values) * head_gain[...], cosine[...], sine[...]
            )
        turned_out[:, window] = values.astype(reduced_precision)


def project(x, gain, blocks, query_gain, key_gain, cosine, sine, heads):
    length, width = x.shape
    count = len(blocks)
    columns = blocks[0].shape[1]
    depth = width // count
    tile = 256

    def rows(size):
        return pl.BlockSpec((tile, size), lambda row: (row, 0))

    def fixed(*shape):
        return pl.BlockSpec(shape, lambda row: (0, 0))

    return pl.pallas_call(
        functools.partial(projecting_kernel, heads, count),
        grid=(length // tile,),
        out_shape=[
            jax.ShapeDtypeStruct((length, width), reduced_precision),
            jax.ShapeDtypeStruct((length, columns - HEAD_DIMENSION), single_precision),
            jax.ShapeDtypeStruct((length, columns), reduced_precision),
        ],
        in_specs=[
            rows(width),
            fixed(1, width),
            fixed(1, HEAD_DIMENSION),
            fixed(1, HEAD_DIMENSION),
            rows(HEAD_DIMENSION),
            rows(HEAD_DIMENSION),
        ]
        + [fixed(depth, columns)] * count,
        out_specs=[rows(width), rows(columns - HEAD_DIMENSION), rows(columns)],
    )(x, gain, query_gain, key_gain, cosine, sine, *blocks)


SCORE_SCALE = HEAD_DIMENSION ** (-0.5)


def allowed_pairs(first, tile, reach, seg_col, seg_row):
    query_place = first + lax.broadcasted_iota(jnp.int32, (tile, reach), 0)
    key_place = lax.broadcasted_iota(jnp.int32, (tile, reach), 1)
    return (key_place <= query_place) & (seg_col[...] == seg_row[:, :reach])


def attending_kernel(blocks, query, key, value, seg_col, seg_row, out, log_total):
    tile = query.shape[0]
    for block in range(blocks):

        @pl.when(pl.program_id(1) == block)
        def _():
            reach = (block + 1) * tile
            scores = contract_last(query[...], key[:reach, :]) * SCORE_SCALE
            allowed = allowed_pairs(block * tile, tile, reach, seg_col, seg_row)
            scores = jnp.where(allowed, scores, -1e30)
            top = jnp.max(scores, axis=1, keepdims=True)
            powers = jnp.exp(scores - top)
            total = jnp.sum(powers, axis=1, keepdims=True)
            probs = (powers * (1.0 / total)).astype(reduced_precision)
            out[...] = matmul(probs, value[:reach, :]).astype(reduced_precision)
            log_total[0] = top + jnp.log(total)


def attend(turned, seg_row, heads):
    length = turned.shape[0]
    tile = 256
    blocks = length // tile
    return pl.pallas_call(
        functools.partial(attending_kernel, blocks),
        grid=(heads, blocks),
        out_shape=[
            jax.ShapeDtypeStruct((length, heads * HEAD_DIMENSION), reduced_precision),
            jax.ShapeDtypeStruct((heads, length, 1), single_precision),
        ],
        in_specs=[
            pl.BlockSpec((tile, HEAD_DIMENSION), lambda head, row: (row, head)),
            pl.BlockSpec((length, HEAD_DIMENSION), lambda head, row: (0, heads)),
            pl.BlockSpec((length, HEAD_DIMENSION), lambda head, row: (0, heads + 1)),
            pl.BlockSpec((tile, 1), lambda head, row: (row, 0)),
            pl.BlockSpec((1, length), lambda head, row: (0, 0)),
        ],
        out_specs=[
            pl.BlockSpec((tile, HEAD_DIMENSION), lambda head, row: (row, head)),
            pl.BlockSpec((1, tile, 1), lambda head, row: (head, row, 0)),
        ],
    )(turned, turned, turned, seg_row[:, None], seg_row[None, :])


def attending_back_kernel(
    heads,
    blocks,
    finish,
    query,
    key,
    value,
    out,
    out_grad,
    log_total,
    seg_col,
    seg_row,
    query_raw,
    key_raw,
    cosine,
    sine,
    query_gain,
    key_gain,
    query_lin,
    key_out,
    value_out,
    query_part,
    key_part,
    key_sum,
    value_sum,
):
    tile = query.shape[0]
    head, row = pl.program_id(0), pl.program_id(1)

    @pl.when((head == 0) & (row == 0))
    def _():
        key_sum[...] = jnp.zeros_like(key_sum)
        value_sum[...] = jnp.zeros_like(value_sum)
        query_part[...] = jnp.zeros_like(query_part)
        key_part[...] = jnp.zeros_like(key_part)

    def backward(grads, raw, cos_part, sin_part, gain):
        turn = unrotate(grads, cos_part, sin_part)
        inverse = inverse_norm(raw)
        hat = raw * inverse
        part = jnp.sum(turn * hat, axis=0, keepdims=True)
        return norm_backward(turn * gain[...], hat, inverse).astype(reduced_precision), part

    for block in range(blocks):

        @pl.when(row == block)
        def _():
            reach = (block + 1) * tile
            window = slice(block * tile, reach)
            queries, grads, keys = query[...], out_grad[...], key[:reach, :]
            scores = contract_last(queries, keys) * SCORE_SCALE
            allowed = allowed_pairs(block * tile, tile, reach, seg_col, seg_row)
            probs = jnp.where(allowed, jnp.exp(scores - log_total[0]), 0.0)
            value_sum[:reach, :] += contract_first(probs.astype(reduced_precision), grads)
            prob_grads = contract_last(grads, value[:reach, :])
            delta = jnp.sum(
                grads.astype(single_precision) * out[...].astype(single_precision),
                axis=1,
                keepdims=True,
            )
            score_grads = (probs * (prob_grads - delta) * SCORE_SCALE).astype(reduced_precision)
            back = matmul(score_grads, keys)
            key_sum[:reach, :] += contract_first(score_grads, queries)
            lin, part = backward(
                back, query_raw[...], cosine[window, :], sine[window, :], query_gain
            )
            query_lin[...] = lin
            query_part[...] += part

    @pl.when((head == heads - 1) & (row == blocks - 1))
    def _():
        if finish:
            lin, part = backward(key_sum[...], key_raw[...], cosine[...], sine[...], key_gain)
            key_out[...] = lin
            key_part[...] = part
        else:
            key_out[...] = key_sum[...]
        value_out[...] = value_sum[...].astype(value_out.dtype)


def attend_back(
    turned, attended, out_grads, log_totals, seg_row, raw, cosine, sine, gains, heads, finish
):
    length = turned.shape[0]
    tile = 256
    blocks = length // tile
    kind = reduced_precision if finish else single_precision
    one_head = pl.BlockSpec((tile, HEAD_DIMENSION), lambda head, row: (row, head))

    def whole(column):
        return pl.BlockSpec((length, HEAD_DIMENSION), lambda head, row: (0, column))

    vector = pl.BlockSpec((1, HEAD_DIMENSION), lambda head, row: (0, 0))
    return pl.pallas_call(
        functools.partial(attending_back_kernel, heads, blocks, finish),
        grid=(heads, blocks),
        out_shape=[
            jax.ShapeDtypeStruct((length, heads * HEAD_DIMENSION), reduced_precision),
            jax.ShapeDtypeStruct((length, HEAD_DIMENSION), kind),
            jax.ShapeDtypeStruct((length, HEAD_DIMENSION), kind),
            jax.ShapeDtypeStruct((1, HEAD_DIMENSION), single_precision),
            jax.ShapeDtypeStruct((1, HEAD_DIMENSION), single_precision),
        ],
        in_specs=[
            one_head,
            whole(heads),
            whole(heads + 1),
            one_head,
            one_head,
            pl.BlockSpec((1, tile, 1), lambda head, row: (head, row, 0)),
            pl.BlockSpec((tile, 1), lambda head, row: (row, 0)),
            pl.BlockSpec((1, length), lambda head, row: (0, 0)),
            one_head,
            whole(heads),
            whole(0),
            whole(0),
            vector,
            vector,
        ],
        out_specs=[one_head, whole(0), whole(0), vector, vector],
        scratch_shapes=[pltpu.VMEM((length, HEAD_DIMENSION), single_precision)] * 2,
    )(
        turned,
        turned,
        turned,
        attended,
        out_grads,
        log_totals,
        seg_row[:, None],
        seg_row[None, :],
        raw,
        raw,
        cosine,
        sine,
        *gains,
    )


def sum_plane(values):
    turn = 1
    while turn < lax.axis_size(SP):
        values = values + flip_permute(values, SP, turn)
        turn = 2 * turn
    return values


def on_device(
    tokens,
    segments,
    prenorm,
    query_proj,
    key_projection,
    value_projection,
    query_norm,
    key_norm_gain,
    output_proj,
    postnorm,
    gate_proj,
    up_proj,
    down_proj,
    out_grad,
):
    token_rows, model_width = tokens.shape
    plane = lax.axis_size(SP)
    lines = lax.axis_size(FSDP)
    spot = lax.axis_index(SP)
    line = lax.axis_index(FSDP)
    seg_row = segments[0]
    heads = QUERY_HEADS // plane
    query_width = heads * HEAD_DIMENSION
    share = max(1, plane // KEY_VALUE_HEADS)
    owned = HEAD_DIMENSION // share
    model_cols = model_width // plane
    ff_cols = gate_proj.shape[1] // plane
    row_block = model_width // lines
    own_place = spot
    if lines == LINE:
        own_place = spot ^ (line * (plane // lines))

    kv_first = (spot // share) * HEAD_DIMENSION
    qkv_slice = jnp.concatenate(
        [
            columns_of(query_proj, spot * query_width, query_width),
            columns_of(key_projection, kv_first, HEAD_DIMENSION),
            columns_of(value_projection, kv_first, HEAD_DIMENSION),
        ],
        axis=1,
    )
    qkv_width = qkv_slice.shape[1]
    both_gains = jnp.pad(
        jnp.stack([prenorm, postnorm]), ((0, 14), (0, qkv_width - row_block))
    )
    qkv_blocks = line_gather(jnp.concatenate([qkv_slice, both_gains], axis=0))
    out_blocks = line_gather(columns_of(output_proj, spot * model_cols, model_cols))
    own_tokens = line_columns(tokens)
    own_grads = line_columns(out_grad)
    everyone = plane_rows(own_tokens)
    grads_all = plane_rows(own_grads)
    gate_up_slice = jnp.concatenate(
        [
            columns_of(gate_proj, spot * ff_cols, ff_cols),
            columns_of(up_proj, spot * ff_cols, ff_cols),
        ],
        axis=1,
    )
    wide_blocks = line_gather(gate_up_slice)
    down_blocks = line_gather(columns_of(down_proj, spot * ff_cols, ff_cols))

    def gain_row(at):
        return jnp.concatenate(
            [block[row_block + at : row_block + at + 1, :row_block] for block in qkv_blocks], axis=1
        ).astype(single_precision)

    prenorm_full, postnorm_full = gain_row(0), gain_row(1)
    cosine, sine = rope_tables(token_places(seg_row))
    query_gain = query_norm.astype(single_precision)[None, :]
    key_gain = key_norm_gain.astype(single_precision)[None, :]
    first_norm, raw, turned = project(
        everyone, prenorm_full, qkv_blocks, query_gain, key_gain, cosine, sine, heads
    )
    attended, log_totals = attend(turned, seg_row, heads)
    (attn_all,) = plane_columns(attended, prenorm_full, False)
    out_cols = jnp.concatenate(out_blocks, axis=0)
    middle_cols = matmul(attn_all, out_cols)
    middle_cols = middle_cols + columns_of(
        everyone, own_place * model_cols, model_cols
    ).astype(single_precision)
    middle_all, second_norm = plane_columns(
        middle_cols.astype(reduced_precision), postnorm_full, True
    )
    middle_own = lax.dynamic_slice_in_dim(middle_all, spot * token_rows, token_rows, 0).astype(
        single_precision
    )
    inv_two_own = inverse_norm(middle_own)
    hat_two_own = middle_own * inv_two_own

    gate_up = jnp.concatenate(wide_blocks, axis=0)
    gate_up_val = matmul(second_norm, gate_up)
    gate_val = gate_up_val[:, :ff_cols]
    up_val = gate_up_val[:, ff_cols:]
    sigmoid_val = jax.nn.sigmoid(gate_val)
    silu_val = gate_val * sigmoid_val
    hidden = (silu_val * up_val).astype(reduced_precision)
    down_parts = row_parts(grads_all, hidden)
    down_cols = jnp.concatenate(down_blocks, axis=0)
    down_cols, *_ = tie(down_cols, *unsummed(down_parts))
    down_sum = line_reduce(down_parts)
    hidden_grad = matmul(grads_all, down_cols)
    gate_grad = (
        hidden_grad * up_val * (sigmoid_val * (1.0 + gate_val * (1.0 - sigmoid_val)))
    ).astype(reduced_precision)
    up_grads = (hidden_grad * silu_val).astype(reduced_precision)
    both_grads = jnp.concatenate([gate_grad, up_grads], axis=1)
    out_pieces, _ = tie(jnp.concatenate(line_order(out_blocks), axis=0), second_norm)
    out_rows = lax.all_to_all(
        out_pieces.reshape(plane, query_width, model_cols),
        SP,
        split_axis=0,
        concat_axis=0,
        tiled=True,
    )
    both_grads, out_rows = tie(both_grads, out_rows)
    norm_two_part = contract_last(both_grads, gate_up).astype(reduced_precision)
    norm_two_grad = plane_reduce(norm_two_part.reshape(plane, token_rows, model_width))
    gate_parts = row_parts(second_norm, both_grads[:, :ff_cols])
    up_parts = row_parts(second_norm, both_grads[:, ff_cols:])
    norm_two_grad, *_ = tie(norm_two_grad, *unsummed(gate_parts), *unsummed(up_parts))
    gate_sum = line_reduce(gate_parts)
    up_sum = line_reduce(up_parts)

    postnorm_part = jnp.sum(norm_two_grad * hat_two_own, axis=0)
    middle_grad = own_grads.astype(single_precision) + norm_backward(
        norm_two_grad * postnorm_full, hat_two_own, inv_two_own
    )
    half = middle_grad.astype(reduced_precision)
    half_all = plane_rows(half)
    late_hidden, _ = tie(hidden, half)
    block_part = contract_last(late_hidden, down_cols).astype(reduced_precision)
    block_out = line_columns(
        (
            middle_own + plane_reduce(block_part.reshape(plane, token_rows, model_width))
        ).astype(reduced_precision)
    )
    out_rows = line_columns(
        jnp.transpose(out_rows.reshape(plane, query_width, model_cols), (1, 0, 2)).reshape(
            query_width, model_width
        )
    )
    attn_grad = contract_last(half_all, out_rows).astype(reduced_precision)
    query_lin, key_lin, value_lin, query_part, key_part = attend_back(
        turned,
        attended,
        attn_grad,
        log_totals,
        seg_row,
        raw,
        cosine,
        sine,
        (query_gain, key_gain),
        heads,
        share == 1,
    )
    qkv = jnp.concatenate([block[:row_block] for block in qkv_blocks], axis=0)
    if share > 1:
        groups = [
            [first + offset for offset in range(share)] for first in range(0, plane, share)
        ]
        both = jnp.concatenate([key_lin, value_lin], axis=1)
        gathered = [both]
        for turn in range(1, share):
            pairs = [
                (group[i], group[(i + turn) % share]) for group in groups for i in range(share)
            ]
            gathered.append(lax.ppermute(both, SP, pairs))
        both = sum(gathered[1:], gathered[0])
        key_sum, value_sum = both[:, :HEAD_DIMENSION], both[:, HEAD_DIMENSION:]
        key_turn = key_sum * cosine - jnp.roll(key_sum, HEAD_DIMENSION // 2, axis=1) * sine
        key_raw = raw[:, query_width:]
        key_inv = inverse_norm(key_raw)
        key_hat = key_raw * key_inv
        key_part = jnp.sum(key_turn * key_hat, axis=0, keepdims=True) / share
        own_first = (spot % share) * owned
        key_lin = columns_of(
            norm_backward(key_turn * key_gain, key_hat, key_inv).astype(reduced_precision),
            own_first,
            owned,
        )
        value_lin = columns_of(value_sum.astype(reduced_precision), own_first, owned)
        qkv = jnp.concatenate(
            [
                qkv[:, :query_width],
                columns_of(qkv, query_width + own_first, owned),
                columns_of(qkv, query_width + HEAD_DIMENSION + own_first, owned),
            ],
            axis=1,
        )
    lin = jnp.concatenate([query_lin, key_lin, value_lin], axis=1)
    qkv_sum = line_reduce(row_parts(first_norm, lin))
    norm_one_part = contract_last(lin, qkv).astype(reduced_precision)
    norm_one_grad = plane_reduce(norm_one_part.reshape(plane, token_rows, model_width))
    out_parts = row_parts(attn_all, columns_of(half_all, own_place * model_cols, model_cols))
    out_sum = line_reduce(out_parts)
    own_tok = own_tokens.astype(single_precision)
    inv_own = inverse_norm(own_tok)
    hat_own = own_tok * inv_own
    prenorm_part = jnp.sum(norm_one_grad * hat_own, axis=0)
    input_grad = (
        middle_grad + norm_backward(norm_one_grad * prenorm_full, hat_own, inv_own)
    ).astype(reduced_precision)
    input_grad = line_columns(input_grad)
    small = sum_plane(
        jnp.concatenate([prenorm_part, postnorm_part, query_part[0], key_part[0]])
    )
    heads_part = small[2 * model_width :]
    small = line_reduce(
        [
            jnp.concatenate(
                [
                    small[at * row_block : (at + 1) * row_block],
                    small[model_width + at * row_block : model_width + (at + 1) * row_block],
                    heads_part,
                ]
            )
            for at in range(lines)
        ],
    )
    grad_prenorm = small[:row_block]
    grad_postnorm = small[row_block : 2 * row_block]
    grad_querynorm = small[2 * row_block : 2 * row_block + HEAD_DIMENSION]
    grad_keynorm = small[2 * row_block + HEAD_DIMENSION :]
    grad_down, grad_gate = spread(jnp.concatenate([down_sum, gate_sum], axis=1), [ff_cols, ff_cols])
    (grad_up,) = spread(up_sum, [ff_cols])
    grad_query, grad_key, grad_value, grad_output = spread(
        jnp.concatenate([qkv_sum, out_sum], axis=1), [query_width, owned, owned, model_cols]
    )
    return (
        block_out,
        input_grad,
        grad_prenorm,
        grad_query,
        grad_key,
        grad_value,
        grad_querynorm,
        grad_keynorm,
        grad_output,
        grad_postnorm,
        grad_gate,
        grad_up,
        grad_down,
    )


def solution(mesh):
    tokens_placed = P((FSDP, SP), None)
    rows, vector = P(FSDP, None), P(FSDP)
    return jax.shard_map(
        on_device,
        mesh=mesh,
        in_specs=(
            tokens_placed,
            rows,
            vector,
            rows,
            rows,
            rows,
            P(),
            P(),
            rows,
            vector,
            rows,
            rows,
            rows,
            tokens_placed,
        ),
        out_specs=(
            tokens_placed,
            tokens_placed,
            vector,
            rows,
            rows,
            rows,
            P(),
            P(),
            rows,
            vector,
            rows,
            rows,
            rows,
        ),
        check_vma=False,
    )
```

```python
import functools

import jax
import jax.numpy as jnp
from jax import lax
from jax.experimental import pallas as pl
from jax.experimental.layout import Layout, with_layout_constraint
from jax.experimental.pallas import tpu as pltpu
from jax.sharding import PartitionSpec as P


QUERY_HEADS = 16
KEY_VALUE_HEADS = 8
HEAD_DIMENSION = 128
LINE = 4
PLANE = 8
FSDP = "fsdp"
SP = "sp"

epsilon = 1e-06
rope_base = 1000000.0
single_precision = jnp.float32
reduced_precision = jnp.bfloat16


def contract_last(left_side, right_side):
    return lax.dot_general(
        left_side, right_side, (((1,), (1,)), ((), ())), preferred_element_type=single_precision
    )


def contract_first(left_side, right_side):
    return lax.dot_general(
        left_side, right_side, (((0,), (0,)), ((), ())), preferred_element_type=single_precision
    )


def matmul(left_side, right_side):
    return jnp.dot(left_side, right_side, preferred_element_type=single_precision)


def tie(*values):
    return lax.optimization_barrier(values)


def rope_tables(places):
    half_dim = HEAD_DIMENSION // 2
    frequency = jnp.power(
        rope_base, -(jnp.arange(half_dim, dtype=single_precision) * (2.0 / HEAD_DIMENSION))
    )
    angles = places[:, None] * frequency[None, :]
    cosine, sine = jnp.cos(angles), jnp.sin(angles)
    return jnp.concatenate([cosine, cosine], axis=1), jnp.concatenate([-sine, sine], axis=1)


def rotate(values, cosine, signed_sine):
    return values * cosine + pltpu.roll(values, HEAD_DIMENSION // 2, 1) * signed_sine


def unrotate(values, cosine, signed_sine):
    return values * cosine - pltpu.roll(values, HEAD_DIMENSION // 2, 1) * signed_sine


def inverse_norm(values):
    return lax.rsqrt(jnp.mean(values * values, axis=-1, keepdims=True) + epsilon)


def norm_backward(grad_hat, normed, inverse):
    return inverse * (grad_hat - normed * jnp.mean(grad_hat * normed, axis=-1, keepdims=True))


def token_places(seg_row):
    doc_starts = jnp.sum((seg_row[None, :] < seg_row[:, None]).astype(jnp.int32), axis=1)
    positions = jnp.arange(seg_row.shape[0], dtype=jnp.int32)
    return (positions - doc_starts).astype(single_precision)


def flip_permute(piece, axis, flip):
    size = lax.axis_size(axis)
    return lax.ppermute(piece, axis, [(i, i ^ flip) for i in range(size)])


def line_order(blocks):
    if len(blocks) != LINE:
        return blocks
    index = lax.axis_index(FSDP)
    odd, high = index % 2 == 1, index // 2 == 1
    near = [jnp.where(odd, blocks[i ^ 1], blocks[i]) for i in range(LINE)]
    return [jnp.where(high, near[i ^ 2], near[i]) for i in range(LINE)]


def line_columns(values):
    lines = lax.axis_size(FSDP)
    if lines != LINE:
        return values
    return jnp.concatenate(line_order(jnp.split(values, lines, axis=1)), axis=1)


def line_gather(piece):
    if lax.axis_size(FSDP) != LINE:
        return list(lax.all_gather(piece, FSDP, axis=0))
    index = lax.axis_index(FSDP)
    second = flip_permute(piece, FSDP, 2)
    first = flip_permute(piece, FSDP, 1)
    inner = lax.ppermute(piece, FSDP, [(1, 2), (2, 1)])
    outer = lax.ppermute(second, FSDP, [(2, 3), (1, 0)])
    third = jnp.where((index == 1) | (index == 2), inner, outer)
    return [piece, first, second, third]


def line_reduce(parts):
    if lax.axis_size(FSDP) != LINE:
        return lax.psum_scatter(jnp.stack(parts), FSDP, scatter_dimension=0, tiled=False)

    def wide(part):
        return part.astype(single_precision)

    kind = parts[0].dtype
    outer = lax.ppermute(parts[3], FSDP, [(3, 2), (0, 1)])
    inner = lax.ppermute(parts[3], FSDP, [(1, 2), (2, 1)])
    first = flip_permute(parts[1], FSDP, 1)
    second = flip_permute((wide(parts[2]) + wide(outer)).astype(kind), FSDP, 2)
    return (wide(parts[0]) + wide(first) + wide(inner) + wide(second)).astype(kind)


def row_parts(left, right):
    parts = []
    for block in jnp.split(left, lax.axis_size(FSDP), axis=1):
        parts.append(contract_first(block, right).astype(reduced_precision))
    return parts


def unsummed(parts):
    return parts[:2] + parts[3:]


def plane_rows(piece):
    return lax.all_gather(piece, SP, axis=0, tiled=True)


def joining_kernel(count, order, *refs):
    pieces, gain, outs = refs[:count], refs[count], refs[count + 1 :]
    whole = jnp.concatenate([piece[0] for piece in pieces], axis=1)
    outs[0][...] = whole
    if len(outs) > 1:
        wide = whole.astype(single_precision)
        outs[1][...] = (wide * inverse_norm(wide) * gain[...]).astype(reduced_precision)


def plane_columns(piece, gain, normed):
    plane, lines = lax.axis_size(SP), lax.axis_size(FSDP)
    pieces = lax.all_gather(piece, SP, axis=0)
    rows, width = piece.shape
    order = jnp.arange(plane, dtype=jnp.int32)
    if lines == LINE:
        order = order ^ (lax.axis_index(FSDP) * (plane // lines))
    tile = 256

    def from_piece(at):
        return pl.BlockSpec((1, tile, width), lambda row, order: (order[at], row, 0))

    whole = pl.BlockSpec((tile, plane * width), lambda row, order: (row, 0))
    count = 2 if normed else 1
    return pl.pallas_call(
        functools.partial(joining_kernel, plane),
        out_shape=[jax.ShapeDtypeStruct((rows, plane * width), piece.dtype)] * count,
        grid_spec=pltpu.PrefetchScalarGridSpec(
            num_scalar_prefetch=1,
            grid=(rows // tile,),
            in_specs=[from_piece(at) for at in range(plane)]
            + [pl.BlockSpec((1, plane * width), lambda row, order: (0, 0))],
            out_specs=[whole] * count,
        ),
    )(order, *[pieces] * plane, gain)


def plane_reduce(parts):
    if lax.axis_size(SP) != PLANE:
        return lax.psum_scatter(parts, SP, scatter_dimension=0, tiled=False).astype(
            single_precision
        )
    index = lax.axis_index(SP)
    chip, core = index // 2, index % 2
    split = parts.reshape((4, 2) + parts.shape[1:])
    given = lax.dynamic_index_in_dim(split, 1 - core, 1, keepdims=False)
    kept = lax.dynamic_index_in_dim(split, core, 1, keepdims=False)
    other = flip_permute(given, SP, 1)
    joined = (kept.astype(single_precision) + other.astype(single_precision)).astype(
        reduced_precision
    )
    total = lax.dynamic_index_in_dim(joined, chip, 0, keepdims=False).astype(single_precision)
    for turn in (1, 2, 3):
        sent = lax.dynamic_index_in_dim(joined, chip ^ turn, 0, keepdims=False)
        found = flip_permute(sent, SP, 2 * turn)
        total = total + found.astype(single_precision)
    return total


def columns_of(weight, first, width):
    return lax.dynamic_slice_in_dim(weight, first, width, 1)


def widening_kernel(widths, piece, *outs):
    offset = 0
    for width, out in zip(widths, outs):
        out[...] = piece[0, :, offset : offset + width].astype(out.dtype)
        offset = offset + width


def spread(reduced, widths):
    size = lax.axis_size(SP)
    rows, total = reduced.shape
    reduced = with_layout_constraint(reduced, Layout(major_to_minor=(0, 1)))
    everything = lax.all_gather(reduced, SP, axis=0)
    tile = 256
    if all(width % 128 == 0 for width in widths) and rows % tile == 0:
        return pl.pallas_call(
            functools.partial(widening_kernel, widths),
            grid=(rows // tile, size),
            out_shape=[
                jax.ShapeDtypeStruct((rows, size * width), single_precision)
                for width in widths
            ],
            in_specs=[pl.BlockSpec((1, tile, total), lambda row, at: (at, row, 0))],
            out_specs=[pl.BlockSpec((tile, width), lambda row, at: (row, at)) for width in widths],
        )(everything)
    results = []
    offset = 0
    for width in widths:
        piece = everything[:, :, offset : offset + width].astype(single_precision)
        results.append(jnp.transpose(piece, (1, 0, 2)).reshape(rows, size * width))
        offset = offset + width
    return results


def choosing_kernel(spot, mine, other, out):
    own = pl.program_id(1) % 2 == spot[0] % 2

    @pl.when(own)
    def _():
        out[...] = mine[0].astype(out.dtype)

    @pl.when(jnp.logical_not(own))
    def _():
        out[...] = other[0].astype(out.dtype)


def spread_direct(reduced):
    size = lax.axis_size(SP)
    rows, width = reduced.shape
    if size != PLANE:
        return spread(reduced, [width])[0]
    found = [reduced]
    for turn in (1, 2, 3):
        found.append(flip_permute(reduced, SP, 2 * turn))
    mine = jnp.stack(found)
    other = flip_permute(mine, SP, 1)
    spot = lax.axis_index(SP).astype(jnp.int32)[None]
    tile = 256
    piece = pl.BlockSpec(
        (1, tile, width), lambda row, at, spot: ((at // 2) ^ (spot[0] // 2), row, 0)
    )
    return pl.pallas_call(
        choosing_kernel,
        out_shape=jax.ShapeDtypeStruct((rows, size * width), single_precision),
        grid_spec=pltpu.PrefetchScalarGridSpec(
            num_scalar_prefetch=1,
            grid=(rows // tile, size),
            in_specs=[piece, piece],
            out_specs=pl.BlockSpec((tile, width), lambda row, at, spot: (row, at)),
        ),
    )(spot, mine, other)


def projecting_kernel(heads, count, x, gain, query_gain, key_gain, cosine, sine, *refs):
    blocks, (normed_out, raw_out, turned_out) = refs[:count], refs[count:]
    wide = x[...].astype(single_precision)
    normed = (wide * inverse_norm(wide) * gain[...]).astype(reduced_precision)
    normed_out[...] = normed
    depth = blocks[0].shape[0]
    total = matmul(normed[:, :depth], blocks[0][...])
    for at in range(1, count):
        total = total + matmul(normed[:, at * depth : (at + 1) * depth], blocks[at][...])
    raw_out[...] = total[:, : (heads + 1) * HEAD_DIMENSION]
    for head in range(heads + 2):
        window = slice(head * HEAD_DIMENSION, (head + 1) * HEAD_DIMENSION)
        values = total[:, window]
        if head <= heads:
            head_gain = query_gain if head < heads else key_gain
            values = rotate(
                values * inverse_norm(values) * head_gain[...], cosine[...], sine[...]
            )
        turned_out[:, window] = values.astype(reduced_precision)


def project(x, gain, blocks, query_gain, key_gain, cosine, sine, heads):
    length, width = x.shape
    count = len(blocks)
    columns = blocks[0].shape[1]
    depth = width // count
    tile = 256

    def rows(size):
        return pl.BlockSpec((tile, size), lambda row: (row, 0))

    def fixed(*shape):
        return pl.BlockSpec(shape, lambda row: (0, 0))

    return pl.pallas_call(
        functools.partial(projecting_kernel, heads, count),
        grid=(length // tile,),
        out_shape=[
            jax.ShapeDtypeStruct((length, width), reduced_precision),
            jax.ShapeDtypeStruct((length, columns - HEAD_DIMENSION), single_precision),
            jax.ShapeDtypeStruct((length, columns), reduced_precision),
        ],
        in_specs=[
            rows(width),
            fixed(1, width),
            fixed(1, HEAD_DIMENSION),
            fixed(1, HEAD_DIMENSION),
            rows(HEAD_DIMENSION),
            rows(HEAD_DIMENSION),
        ]
        + [fixed(depth, columns)] * count,
        out_specs=[rows(width), rows(columns - HEAD_DIMENSION), rows(columns)],
    )(x, gain, query_gain, key_gain, cosine, sine, *blocks)


SCORE_SCALE = HEAD_DIMENSION ** (-0.5)


def allowed_pairs(first, tile, reach, seg_col, seg_row):
    query_place = first + lax.broadcasted_iota(jnp.int32, (tile, reach), 0)
    key_place = lax.broadcasted_iota(jnp.int32, (tile, reach), 1)
    return (key_place <= query_place) & (seg_col[...] == seg_row[:, :reach])


def attending_kernel(blocks, query, key, value, seg_col, seg_row, out, log_total):
    tile = query.shape[0]
    for block in range(blocks):

        @pl.when(pl.program_id(1) == block)
        def _():
            reach = (block + 1) * tile
            scores = contract_last(query[...], key[:reach, :]) * SCORE_SCALE
            allowed = allowed_pairs(block * tile, tile, reach, seg_col, seg_row)
            scores = jnp.where(allowed, scores, -1e30)
            top = jnp.max(scores, axis=1, keepdims=True)
            powers = jnp.exp(scores - top)
            total = jnp.sum(powers, axis=1, keepdims=True)
            probs = (powers * (1.0 / total)).astype(reduced_precision)
            out[...] = matmul(probs, value[:reach, :]).astype(reduced_precision)
            log_total[0] = top + jnp.log(total)


def attend(turned, seg_row, heads):
    length = turned.shape[0]
    tile = 256
    blocks = length // tile
    return pl.pallas_call(
        functools.partial(attending_kernel, blocks),
        grid=(heads, blocks),
        out_shape=[
            jax.ShapeDtypeStruct((length, heads * HEAD_DIMENSION), reduced_precision),
            jax.ShapeDtypeStruct((heads, length, 1), single_precision),
        ],
        in_specs=[
            pl.BlockSpec((tile, HEAD_DIMENSION), lambda head, row: (row, head)),
            pl.BlockSpec((length, HEAD_DIMENSION), lambda head, row: (0, heads)),
            pl.BlockSpec((length, HEAD_DIMENSION), lambda head, row: (0, heads + 1)),
            pl.BlockSpec((tile, 1), lambda head, row: (row, 0)),
            pl.BlockSpec((1, length), lambda head, row: (0, 0)),
        ],
        out_specs=[
            pl.BlockSpec((tile, HEAD_DIMENSION), lambda head, row: (row, head)),
            pl.BlockSpec((1, tile, 1), lambda head, row: (head, row, 0)),
        ],
    )(turned, turned, turned, seg_row[:, None], seg_row[None, :])


def attending_back_kernel(
    heads,
    blocks,
    finish,
    query,
    key,
    value,
    out,
    out_grad,
    log_total,
    seg_col,
    seg_row,
    query_raw,
    key_raw,
    cosine,
    sine,
    query_gain,
    key_gain,
    query_lin,
    key_out,
    value_out,
    query_part,
    key_part,
    key_sum,
    value_sum,
):
    tile = query.shape[0]
    head, row = pl.program_id(0), pl.program_id(1)

    @pl.when((head == 0) & (row == 0))
    def _():
        key_sum[...] = jnp.zeros_like(key_sum)
        value_sum[...] = jnp.zeros_like(value_sum)
        query_part[...] = jnp.zeros_like(query_part)
        key_part[...] = jnp.zeros_like(key_part)

    def backward(grads, raw, cos_part, sin_part, gain):
        turn = unrotate(grads, cos_part, sin_part)
        inverse = inverse_norm(raw)
        hat = raw * inverse
        part = jnp.sum(turn * hat, axis=0, keepdims=True)
        return norm_backward(turn * gain[...], hat, inverse).astype(reduced_precision), part

    for block in range(blocks):

        @pl.when(row == block)
        def _():
            reach = (block + 1) * tile
            window = slice(block * tile, reach)
            queries, grads, keys = query[...], out_grad[...], key[:reach, :]
            scores = contract_last(queries, keys) * SCORE_SCALE
            allowed = allowed_pairs(block * tile, tile, reach, seg_col, seg_row)
            probs = jnp.where(allowed, jnp.exp(scores - log_total[0]), 0.0)
            value_sum[:reach, :] += contract_first(probs.astype(reduced_precision), grads)
            prob_grads = contract_last(grads, value[:reach, :])
            delta = jnp.sum(
                grads.astype(single_precision) * out[...].astype(single_precision),
                axis=1,
                keepdims=True,
            )
            score_grads = (probs * (prob_grads - delta) * SCORE_SCALE).astype(reduced_precision)
            back = matmul(score_grads, keys)
            key_sum[:reach, :] += contract_first(score_grads, queries)
            lin, part = backward(
                back, query_raw[...], cosine[window, :], sine[window, :], query_gain
            )
            query_lin[...] = lin
            query_part[...] += part

    @pl.when((head == heads - 1) & (row == blocks - 1))
    def _():
        if finish:
            lin, part = backward(key_sum[...], key_raw[...], cosine[...], sine[...], key_gain)
            key_out[...] = lin
            key_part[...] = part
        else:
            key_out[...] = key_sum[...]
        value_out[...] = value_sum[...].astype(value_out.dtype)


def attend_back(
    turned, attended, out_grads, log_totals, seg_row, raw, cosine, sine, gains, heads, finish
):
    length = turned.shape[0]
    tile = 256
    blocks = length // tile
    kind = reduced_precision if finish else single_precision
    one_head = pl.BlockSpec((tile, HEAD_DIMENSION), lambda head, row: (row, head))

    def whole(column):
        return pl.BlockSpec((length, HEAD_DIMENSION), lambda head, row: (0, column))

    vector = pl.BlockSpec((1, HEAD_DIMENSION), lambda head, row: (0, 0))
    return pl.pallas_call(
        functools.partial(attending_back_kernel, heads, blocks, finish),
        grid=(heads, blocks),
        out_shape=[
            jax.ShapeDtypeStruct((length, heads * HEAD_DIMENSION), reduced_precision),
            jax.ShapeDtypeStruct((length, HEAD_DIMENSION), kind),
            jax.ShapeDtypeStruct((length, HEAD_DIMENSION), kind),
            jax.ShapeDtypeStruct((1, HEAD_DIMENSION), single_precision),
            jax.ShapeDtypeStruct((1, HEAD_DIMENSION), single_precision),
        ],
        in_specs=[
            one_head,
            whole(heads),
            whole(heads + 1),
            one_head,
            one_head,
            pl.BlockSpec((1, tile, 1), lambda head, row: (head, row, 0)),
            pl.BlockSpec((tile, 1), lambda head, row: (row, 0)),
            pl.BlockSpec((1, length), lambda head, row: (0, 0)),
            one_head,
            whole(heads),
            whole(0),
            whole(0),
            vector,
            vector,
        ],
        out_specs=[one_head, whole(0), whole(0), vector, vector],
        scratch_shapes=[pltpu.VMEM((length, HEAD_DIMENSION), single_precision)] * 2,
    )(
        turned,
        turned,
        turned,
        attended,
        out_grads,
        log_totals,
        seg_row[:, None],
        seg_row[None, :],
        raw,
        raw,
        cosine,
        sine,
        *gains,
    )


def sum_plane(values):
    turn = 1
    while turn < lax.axis_size(SP):
        values = values + flip_permute(values, SP, turn)
        turn = 2 * turn
    return values


def on_device(
    tokens,
    segments,
    prenorm,
    query_proj,
    key_projection,
    value_projection,
    query_norm,
    key_norm_gain,
    output_proj,
    postnorm,
    gate_proj,
    up_proj,
    down_proj,
    out_grad,
):
    token_rows, model_width = tokens.shape
    plane = lax.axis_size(SP)
    lines = lax.axis_size(FSDP)
    spot = lax.axis_index(SP)
    line = lax.axis_index(FSDP)
    seg_row = segments[0]
    heads = QUERY_HEADS // plane
    query_width = heads * HEAD_DIMENSION
    share = max(1, plane // KEY_VALUE_HEADS)
    owned = HEAD_DIMENSION // share
    model_cols = model_width // plane
    ff_cols = gate_proj.shape[1] // plane
    row_block = model_width // lines
    own_place = spot
    if lines == LINE:
        own_place = spot ^ (line * (plane // lines))

    kv_first = (spot // share) * HEAD_DIMENSION
    qkv_slice = jnp.concatenate(
        [
            columns_of(query_proj, spot * query_width, query_width),
            columns_of(key_projection, kv_first, HEAD_DIMENSION),
            columns_of(value_projection, kv_first, HEAD_DIMENSION),
        ],
        axis=1,
    )
    qkv_width = qkv_slice.shape[1]
    both_gains = jnp.pad(
        jnp.stack([prenorm, postnorm]), ((0, 14), (0, qkv_width - row_block))
    )
    qkv_blocks = line_gather(jnp.concatenate([qkv_slice, both_gains], axis=0))
    out_blocks = line_gather(columns_of(output_proj, spot * model_cols, model_cols))
    own_tokens = line_columns(tokens)
    own_grads = line_columns(out_grad)
    everyone = plane_rows(own_tokens)
    grads_all = plane_rows(own_grads)
    gate_up_slice = jnp.concatenate(
        [
            columns_of(gate_proj, spot * ff_cols, ff_cols),
            columns_of(up_proj, spot * ff_cols, ff_cols),
        ],
        axis=1,
    )
    wide_blocks = line_gather(gate_up_slice)
    down_blocks = line_gather(columns_of(down_proj, spot * ff_cols, ff_cols))

    def gain_row(at):
        return jnp.concatenate(
            [block[row_block + at : row_block + at + 1, :row_block] for block in qkv_blocks], axis=1
        ).astype(single_precision)

    prenorm_full, postnorm_full = gain_row(0), gain_row(1)
    cosine, sine = rope_tables(token_places(seg_row))
    query_gain = query_norm.astype(single_precision)[None, :]
    key_gain = key_norm_gain.astype(single_precision)[None, :]
    first_norm, raw, turned = project(
        everyone, prenorm_full, qkv_blocks, query_gain, key_gain, cosine, sine, heads
    )
    attended, log_totals = attend(turned, seg_row, heads)
    (attn_all,) = plane_columns(attended, prenorm_full, False)
    out_cols = jnp.concatenate(out_blocks, axis=0)
    middle_cols = matmul(attn_all, out_cols)
    middle_cols = middle_cols + columns_of(
        everyone, own_place * model_cols, model_cols
    ).astype(single_precision)
    middle_all, second_norm = plane_columns(
        middle_cols.astype(reduced_precision), postnorm_full, True
    )
    middle_own = lax.dynamic_slice_in_dim(middle_all, spot * token_rows, token_rows, 0).astype(
        single_precision
    )
    inv_two_own = inverse_norm(middle_own)
    hat_two_own = middle_own * inv_two_own

    gate_up = jnp.concatenate(wide_blocks, axis=0)
    gate_up_val = matmul(second_norm, gate_up)
    gate_val = gate_up_val[:, :ff_cols]
    up_val = gate_up_val[:, ff_cols:]
    sigmoid_val = jax.nn.sigmoid(gate_val)
    silu_val = gate_val * sigmoid_val
    hidden = (silu_val * up_val).astype(reduced_precision)
    down_parts = row_parts(grads_all, hidden)
    down_cols = jnp.concatenate(down_blocks, axis=0)
    down_cols, *_ = tie(down_cols, *unsummed(down_parts))
    down_sum = line_reduce(down_parts)
    hidden_grad = matmul(grads_all, down_cols)
    gate_grad = (
        hidden_grad * up_val * (sigmoid_val * (1.0 + gate_val * (1.0 - sigmoid_val)))
    ).astype(reduced_precision)
    up_grads = (hidden_grad * silu_val).astype(reduced_precision)
    both_grads = jnp.concatenate([gate_grad, up_grads], axis=1)
    out_pieces, _ = tie(jnp.concatenate(line_order(out_blocks), axis=0), both_grads)
    out_rows = lax.all_to_all(
        out_pieces.reshape(plane, query_width, model_cols),
        SP,
        split_axis=0,
        concat_axis=0,
        tiled=True,
    )
    norm_two_part = contract_last(both_grads, gate_up).astype(reduced_precision)
    norm_two_part, out_rows = tie(norm_two_part, out_rows)
    norm_two_grad = plane_reduce(norm_two_part.reshape(plane, token_rows, model_width))
    gate_parts = row_parts(second_norm, both_grads[:, :ff_cols])
    up_parts = row_parts(second_norm, both_grads[:, ff_cols:])
    norm_two_grad, *_ = tie(norm_two_grad, *unsummed(gate_parts), *unsummed(up_parts))
    gate_sum = line_reduce(gate_parts)
    up_sum = line_reduce(up_parts)

    postnorm_part = jnp.sum(norm_two_grad * hat_two_own, axis=0)
    middle_grad = own_grads.astype(single_precision) + norm_backward(
        norm_two_grad * postnorm_full, hat_two_own, inv_two_own
    )
    half = middle_grad.astype(reduced_precision)
    half_all = plane_rows(half)
    block_part = contract_last(hidden, down_cols).astype(reduced_precision)
    block_out = line_columns(
        (
            middle_own + plane_reduce(block_part.reshape(plane, token_rows, model_width))
        ).astype(reduced_precision)
    )
    out_rows = line_columns(
        jnp.transpose(out_rows.reshape(plane, query_width, model_cols), (1, 0, 2)).reshape(
            query_width, model_width
        )
    )
    attn_grad = contract_last(half_all, out_rows).astype(reduced_precision)
    query_lin, key_lin, value_lin, query_part, key_part = attend_back(
        turned,
        attended,
        attn_grad,
        log_totals,
        seg_row,
        raw,
        cosine,
        sine,
        (query_gain, key_gain),
        heads,
        share == 1,
    )
    qkv = jnp.concatenate([block[:row_block] for block in qkv_blocks], axis=0)
    if share > 1:
        groups = [
            [first + offset for offset in range(share)] for first in range(0, plane, share)
        ]
        both = jnp.concatenate([key_lin, value_lin], axis=1)
        gathered = [both]
        for turn in range(1, share):
            pairs = [
                (group[i], group[(i + turn) % share]) for group in groups for i in range(share)
            ]
            gathered.append(lax.ppermute(both, SP, pairs))
        both = sum(gathered[1:], gathered[0])
        key_sum, value_sum = both[:, :HEAD_DIMENSION], both[:, HEAD_DIMENSION:]
        key_turn = key_sum * cosine - jnp.roll(key_sum, HEAD_DIMENSION // 2, axis=1) * sine
        key_raw = raw[:, query_width:]
        key_inv = inverse_norm(key_raw)
        key_hat = key_raw * key_inv
        key_part = jnp.sum(key_turn * key_hat, axis=0, keepdims=True) / share
        own_first = (spot % share) * owned
        key_lin = columns_of(
            norm_backward(key_turn * key_gain, key_hat, key_inv).astype(reduced_precision),
            own_first,
            owned,
        )
        value_lin = columns_of(value_sum.astype(reduced_precision), own_first, owned)
        qkv = jnp.concatenate(
            [
                qkv[:, :query_width],
                columns_of(qkv, query_width + own_first, owned),
                columns_of(qkv, query_width + HEAD_DIMENSION + own_first, owned),
            ],
            axis=1,
        )
    lin = jnp.concatenate([query_lin, key_lin, value_lin], axis=1)
    qkv_sum = line_reduce(row_parts(first_norm, lin))
    norm_one_part = contract_last(lin, qkv).astype(reduced_precision)
    norm_one_grad = plane_reduce(norm_one_part.reshape(plane, token_rows, model_width))
    out_parts = row_parts(attn_all, columns_of(half_all, own_place * model_cols, model_cols))
    out_sum = line_reduce(out_parts)
    own_tok = own_tokens.astype(single_precision)
    inv_own = inverse_norm(own_tok)
    hat_own = own_tok * inv_own
    prenorm_part = jnp.sum(norm_one_grad * hat_own, axis=0)
    input_grad = (
        middle_grad + norm_backward(norm_one_grad * prenorm_full, hat_own, inv_own)
    ).astype(reduced_precision)
    input_grad = line_columns(input_grad)
    small = sum_plane(
        jnp.concatenate([prenorm_part, postnorm_part, query_part[0], key_part[0]])
    )
    heads_part = small[2 * model_width :]
    small = line_reduce(
        [
            jnp.concatenate(
                [
                    small[at * row_block : (at + 1) * row_block],
                    small[model_width + at * row_block : model_width + (at + 1) * row_block],
                    heads_part,
                ]
            )
            for at in range(lines)
        ],
    )
    grad_prenorm = small[:row_block]
    grad_postnorm = small[row_block : 2 * row_block]
    grad_querynorm = small[2 * row_block : 2 * row_block + HEAD_DIMENSION]
    grad_keynorm = small[2 * row_block + HEAD_DIMENSION :]
    grad_down = spread_direct(down_sum)
    grad_gate = spread_direct(gate_sum)
    (grad_up,) = spread(up_sum, [ff_cols])
    grad_query, grad_key, grad_value, grad_output = spread(
        jnp.concatenate([qkv_sum, out_sum], axis=1), [query_width, owned, owned, model_cols]
    )
    return (
        block_out,
        input_grad,
        grad_prenorm,
        grad_query,
        grad_key,
        grad_value,
        grad_querynorm,
        grad_keynorm,
        grad_output,
        grad_postnorm,
        grad_gate,
        grad_up,
        grad_down,
    )


def solution(mesh):
    tokens_placed = P((FSDP, SP), None)
    rows, vector = P(FSDP, None), P(FSDP)
    return jax.shard_map(
        on_device,
        mesh=mesh,
        in_specs=(
            tokens_placed,
            rows,
            vector,
            rows,
            rows,
            rows,
            P(),
            P(),
            rows,
            vector,
            rows,
            rows,
            rows,
            tokens_placed,
        ),
        out_specs=(
            tokens_placed,
            tokens_placed,
            vector,
            rows,
            rows,
            rows,
            P(),
            P(),
            rows,
            vector,
            rows,
            rows,
            rows,
        ),
        check_vma=False,
    )
```
